128 devices in a mesh: row: 16 (over x_lo, y, core), col: 8 (over x_hi, z).
Axes of the slice: x: 4 (x_hi: 2, x_lo: 2; x = x_hi * 2 + x_lo), y: 4, z: 4, core: 2. Of those that a mesh axis runs over, the one named last changes fastest.
Arguments:
- nodes: bfloat16 [32768, 256], P(('row', 'col')), may hold values from -6 to 6
- weight: bfloat16 [256, 256], replicated, may hold values from -0.375 to 0.375
- adjacency: bfloat16 [32768, 32768], P('row', 'col'), may hold values from -0.046875 to 0.046875
- history: bfloat16 [131072, 256], P(('row', 'col')), may hold values from -6 to 6
- pull_owner: int32 [4096, 1], P(('row', 'col')), may hold values from 0 to 15; in each aligned block of 32 rows (0 to 31, 32 to 63, ...) at most 4 rows name the same one
- pull_slot: int32 [4096], P(('row', 'col')), may hold values from 0 to 7
- pull_target: int32 [4096], P(('row', 'col')), may hold values from 0 to 15
- hist_tiles: bfloat16 [4096, 128, 128], P(('row', 'col')), may hold values from -0.375 to 0.375
- cotangent: bfloat16 [32768, 256], P(('row', 'col')), may hold values from -6 to 6
Outputs:
- activated: bfloat16 [32768, 256], P(('row', 'col'))
- grad_nodes: bfloat16 [32768, 256], P(('row', 'col'))
- grad_weight: float32 [256, 256], replicated
The draws below stay inside these ranges and needn't reach their ends.
Inputs may be any that keep to these rules, and one draw needn't show every extreme that they name: `pull_owner`: among the 32 pulls of one device no owner is named more than 4 times, a bound that some block reaches.
All inputs are finite; a program needn't handle non-finite values.
Results may differ from the reference program's by a relative error of at most 0.029.
Values may be sent and summed in bfloat16 or wider, within the bound.
A program may use at most 128 MiB of HBM per device.

```python
import math
import jax
import jax.numpy as jnp
import numpy as np
from jax import lax

HID = 256
BLK = 128
N_DEV = 256
K = 32
CAP = 4
HB_DEV = 8
NODES = 32768
N_ROW = 16
N_COL = 8
DEVICES = 128


def touch_ends(drawn, key, low, largest):
    longest = drawn.shape.index(max(drawn.shape))
    spots = []
    for shift in (0, 1):
        where = [jax.random.randint(jax.random.fold_in(key, axis), (), 0, length) for axis, length in enumerate(drawn.shape)]
        where[longest] = (where[longest] + shift) % drawn.shape[longest]
        spots.append(tuple(where))
    return drawn.at[spots[0]].set(low).at[spots[1]].set(largest)


def raised(array, key, source, target, blocks, factor):
    def block_of(position):
        return (jnp.arange(array.shape[position]) // (array.shape[position] // blocks)).reshape((-1,) + (1,) * (array.ndim - 1 - position))

    near = jax.random.permutation(key, blocks)[block_of(target)]
    far = (block_of(target) + blocks // 2) % blocks
    return jnp.where((block_of(source) == near) | (block_of(source) == far), factor * array, array)


def level_of(rng, extent, shards, least, high):
    def one(axis_at, parts):
        draws = jax.random.uniform(jax.random.fold_in(jax.random.fold_in(rng, 6), axis_at), (parts,), jnp.float32, least / len(shards), high / len(shards))
        return jnp.repeat(jnp.exp(draws), extent[axis_at] // parts).reshape((-1,) + (1,) * (len(extent) - axis_at - 1))

    level = one(*shards[0])
    for cut in shards[1:]:
        level = level * one(*cut)
    return level


def shared_out(key, own, number, rows, amount, top, most, slope):
    ranking = jax.random.permutation(key, amount)
    packed, ordinary = portions_of(amount, rows * top, most, slope, True), portions_of(amount, rows * top, most, slope, False)
    places = jnp.arange(amount)

    def named(lengths, offset_by):
        used = int((lengths > 0).sum())
        fixed = max(1, used // 4)
        passed = fixed + (places - fixed + offset_by * (used - fixed)) % max(1, amount - fixed)
        return jnp.zeros((amount,), jnp.int32).at[ranking[jnp.where(places < fixed, places, passed)]].set(jnp.asarray(lengths, jnp.int32))

    lengths = jnp.where(number % 4 == 0, named(packed, number // 4), named(ordinary, number - number // 4 - 1))
    mixed = jax.random.permutation(jax.random.fold_in(own, 3), amount)
    giver, taker = mixed[0:amount // 2 * 2:2], mixed[1:amount // 2 * 2:2]
    slack = jnp.minimum(lengths[giver] - 1, most - lengths[taker]) // 2
    slack = jnp.where((giver == ranking[0]) | (taker == ranking[0]) | (lengths[taker] == 0), 0, jnp.maximum(slack, 0))
    passed = jax.random.randint(jax.random.fold_in(own, 4), (amount // 2,), 0, 1 << 20) % (slack + 1)
    lengths = lengths.at[giver].add(-passed).at[taker].add(passed)
    items = jnp.searchsorted(jnp.cumsum(lengths), jnp.arange(rows * top), side="right").astype(jnp.int32)
    table = items.reshape(top, rows).T
    table = table[jax.random.permutation(jax.random.fold_in(own, 1), rows)]
    offset_by = jax.random.randint(jax.random.fold_in(own, 2), (rows, 1), 0, top)
    return jnp.take_along_axis(table, (jnp.arange(top)[None, :] + offset_by) % top, axis=1)


def portions_of(amount, total, reach, skew, full):
    portions = [(1 << 20) // math.isqrt(rank ** skew) + 1 for rank in range(1, amount + 1)]
    largest = reach if full else min(reach, max(-(-total // amount), total * portions[0] // sum(portions)))
    least = 1 if total - largest >= amount - 1 else 0
    holding, surplus = [largest] + [least] * (amount - 1), total - largest - least * (amount - 1)
    while surplus > 0:
        candidates = [i for i in range(1, amount) if holding[i] < largest] or [i for i in range(1, amount) if holding[i] < reach]
        pool, remaining = sum([portions[i] for i in candidates]), surplus
        for i in candidates:
            extra = min(reach - holding[i], max(1, remaining * portions[i] // pool), surplus)
            holding[i] = holding[i] + extra
            surplus = surplus - extra
    return np.array(holding)


def normal_values(own_key, extent, spread, bound, cuts=(), kind=jnp.bfloat16):
    factor_of = level_of(own_key, extent, cuts, -0.22, 0.18) if cuts else 1.0
    values = jax.random.normal(own_key, extent, jnp.float32) * spread * factor_of
    return jnp.minimum(jnp.maximum(values, -bound), bound).astype(kind)


def noise_with(own_key, dims, spread, limit, shards, heavy, held_as=jnp.bfloat16):
    values = spread * jax.random.normal(own_key, dims, jnp.float32)
    if shards:
        values = values * level_of(own_key, dims, shards, -0.22, 0.18)
    return jnp.clip(raised(values, jax.random.fold_in(own_key, 3), *heavy), -limit, limit).astype(held_as)


def setup_inputs(seed: int = 0) -> dict:
    arg_keys = jax.random.split(jax.random.key(seed), 10)
    nodes = normal_values(arg_keys[0], (NODES, HID), 1.0, 6.0, ((0, 128),))
    weight = normal_values(arg_keys[1], (HID, HID), HID ** -0.5, 0.375)
    adjacency = noise_with(arg_keys[2], (NODES, NODES), NODES ** -0.5, 0.046875, ((0, 16), (1, 8)), (1, 0, 16, 2.0))
    history = normal_values(arg_keys[3], (DEVICES * HB_DEV * BLK, HID), 1.0, 6.0, ((0, 128),))
    pull_owner_keys = jax.random.split(jax.random.fold_in(arg_keys[4], 1), (DEVICES * K) // K)
    pull_owner_turns = jax.random.permutation(jax.random.fold_in(arg_keys[4], 3), (DEVICES * K) // K)
    pull_owner = jax.vmap(lambda own, number: shared_out(jax.random.fold_in(arg_keys[4], 2), own, number, K, N_ROW, 1, CAP, 2))(pull_owner_keys, pull_owner_turns).reshape((DEVICES * K, 1))
    pull_slot = touch_ends(jax.random.randint(arg_keys[5], (DEVICES * K,), 0, HB_DEV), jax.random.fold_in(arg_keys[5], 1), 0, HB_DEV - 1).astype(jnp.int32)
    pull_target = touch_ends(jax.random.randint(arg_keys[6], (DEVICES * K,), 0, NODES // N_ROW // BLK), jax.random.fold_in(arg_keys[6], 1), 0, (NODES // N_ROW // BLK) - 1).astype(jnp.int32)
    hist_tiles = normal_values(arg_keys[7], (DEVICES * K, BLK, BLK), (2 * BLK) ** -0.5, 0.375, ((0, 128),))
    cotangent = normal_values(arg_keys[8], (NODES, HID), 1.0, 6.0, ((0, 128),))
    return {"nodes": nodes, "weight": weight, "adjacency": adjacency, "history": history, "pull_owner": pull_owner, "pull_slot": pull_slot, "pull_target": pull_target, "hist_tiles": hist_tiles, "cotangent": cotangent}


def reference(nodes, weight, adjacency, history, pull_owner, pull_slot, pull_target, hist_tiles, cotangent):
    projected = jnp.dot(nodes, weight, preferred_element_type=jnp.float32).astype(jnp.bfloat16)
    permuted = projected.reshape(N_ROW, N_COL, N_DEV, HID).transpose(1, 0, 2, 3).reshape(NODES, HID)
    panel_rows = NODES // N_ROW
    row_count = panel_rows // BLK
    blocks = history.reshape(N_ROW, N_COL, HB_DEV, BLK, HID)
    owners = pull_owner[:, 0].reshape(DEVICES, K)
    slot_ids = pull_slot.reshape(DEVICES, K)
    targets = pull_target.reshape(DEVICES, K)
    tiles_all = hist_tiles.reshape(DEVICES, K, BLK, BLK)

    def one_device(accum, device):
        row_index = device // N_COL
        col_index = device % N_COL
        fetched = blocks[owners[device], col_index, slot_ids[device]]
        products = jnp.einsum('kab,kbf->kaf', tiles_all[device].astype(jnp.float32), fetched.astype(jnp.float32), precision=lax.Precision.HIGHEST)
        placing = (targets[device][None, :] == jnp.arange(row_count, dtype=jnp.int32)[:, None]).astype(jnp.float32)
        term = jnp.einsum('jk,kaf->jaf', placing, products, precision=lax.Precision.HIGHEST).reshape(panel_rows, HID)
        begin = (row_index * panel_rows).astype(jnp.int32)
        current = lax.dynamic_slice_in_dim(accum, begin, panel_rows, 0)
        return (lax.dynamic_update_slice_in_dim(accum, current + term, begin, 0), None)
    history_term, _ = lax.scan(one_device, jnp.zeros((NODES, HID), jnp.float32), jnp.arange(DEVICES, dtype=jnp.int32))
    permuted_f = permuted.astype(jnp.float32)
    adjacency_panels = adjacency.reshape(N_ROW, panel_rows, NODES)

    def forward_panel(row_slab):
        return jnp.dot(row_slab.astype(jnp.float32), permuted_f, precision=lax.Precision.HIGHEST)
    mixed = lax.map(forward_panel, adjacency_panels).reshape(NODES, HID) + history_term
    activated = jax.nn.silu(mixed).astype(jnp.bfloat16)
    sigmoid_z = jax.nn.sigmoid(mixed)
    grad_pre = (cotangent.astype(jnp.float32) * sigmoid_z * (1.0 + mixed * (1.0 - sigmoid_z))).astype(jnp.bfloat16)
    grad_panels = grad_pre.reshape(N_ROW, panel_rows, HID)

    def backward_panel(accum, pieces):
        row_slab, grad_slab = pieces
        return (accum + jnp.dot(row_slab.astype(jnp.float32).T, grad_slab.astype(jnp.float32), precision=lax.Precision.HIGHEST), None)
    grad_perm, _ = lax.scan(backward_panel, jnp.zeros((NODES, HID), jnp.float32), (adjacency_panels, grad_panels))
    grad_proj = grad_perm.astype(jnp.bfloat16).reshape(N_COL, N_ROW, N_DEV, HID).transpose(1, 0, 2, 3).reshape(NODES, HID)
    grad_nodes = jnp.dot(grad_proj, weight.T, preferred_element_type=jnp.float32).astype(jnp.bfloat16)
    grad_weight = jnp.dot(nodes.astype(jnp.float32).T, grad_proj.astype(jnp.float32), precision=lax.Precision.HIGHEST) / math.sqrt(NODES)
    return (activated, grad_nodes, grad_weight)
```

```python
import math

import jax
import jax.numpy as jnp
from jax import lax
from jax.experimental import pallas as pl
from jax.experimental.pallas import tpu as pltpu
from jax.sharding import PartitionSpec as P

HID = 256
BLK = 128
HALF = 128
NR = 16
NC = 8
SPAN = 256
K = 32
MESH = pl.DeviceIdType.MESH
F32 = jnp.float32
BF16 = jnp.bfloat16


def kernel(
    chain_ref, owner_ref, slot_ref, nodes_hbm, w_hbm, adj_hbm, hist_hbm, tiles_hbm, cot_hbm,
    act_ref, gn_ref, gw_ref,
    nodes_all, hist0, hist1, adj, w, cot, tiles, proj, inb, sums,
    rs_snd, rs_rcv, gt, out_t, sib_snd, sib_rcv, d_snd, d_rcv,
    gwt, gw_rcv1, gw_sum, gw_rcv2, gw_all,
    loc_sem, snd_sem, ag_sem, rs_sem, g_sem, sib_sem, d_sem, gw1_sem, gw2_sem, gw3_sem,
):
    r = lax.axis_index("row")
    c = lax.axis_index("col")
    core = r % 2
    chip = r // 2
    x = chip // 4
    y = chip % 4
    other = 1 - x
    up = (y + 1) % 4
    down = (y + 3) % 4
    far = (y + 2) % 4
    sib = r + 1 - 2 * core

    def row_of(xx, yy, kk):
        return (xx * 4 + yy) * 2 + kk

    hist = (hist0, hist1)
    sent = []

    def send(src, dst, rsem, row, col):
        copy = pltpu.make_async_remote_copy(
            src_ref=src, dst_ref=dst, send_sem=snd_sem.at[len(sent)], recv_sem=rsem,
            device_id=(row, col), device_id_type=MESH,
        )
        copy.start()
        sent.append(copy)

    def arrive(dst, rsem):
        pltpu.make_async_remote_copy(
            src_ref=dst, dst_ref=dst, send_sem=snd_sem.at[0], recv_sem=rsem,
            device_id=(sib, c), device_id_type=MESH,
        ).wait_recv()

    def local(src, dst, i):
        copy = pltpu.make_async_copy(src, dst, loc_sem.at[i])
        copy.start()
        return copy

    own_nodes = local(nodes_hbm, nodes_all.at[r], 0)
    own_hist = [
        local(hist_hbm.at[:, :, pl.ds(h * HALF, HALF)], hist[h].at[pl.ds(r * 8, 8)], 1 + h)
        for h in range(2)
    ]
    w_copy = local(w_hbm, w, 3)
    adj_copy = local(adj_hbm, adj, 4)
    tiles_copy = local(tiles_hbm, tiles, 5)
    cot_copy = local(cot_hbm, cot, 6)

    barrier = pltpu.get_barrier_semaphore()
    for d in range(1, NR):
        pl.semaphore_signal(barrier, inc=1, device_id=((r + d) % NR, c), device_id_type=MESH)
    for d in range(1, NC):
        pl.semaphore_signal(barrier, inc=1, device_id=(r, (c + d) % NC), device_id_type=MESH)
    pl.semaphore_wait(barrier, NR + NC - 2)

    def piece(chunk, owner, part):
        if chunk == 0:
            ref = nodes_all.at[owner]
            return ref if part is None else ref.at[pl.ds(part * 128, 128)]
        if part is None:
            return hist[chunk - 1].at[pl.ds(owner * 8, 8)]
        return hist[chunk - 1].at[pl.ds(owner * 8 + part * 4, 4)]

    def push(chunk, owner, part, dest):
        ref = piece(chunk, owner, part)
        send(ref, ref, ag_sem.at[chunk, owner, part or 0], dest, c)

    def got(chunk, owner, part=None):
        arrive(piece(chunk, owner, part), ag_sem.at[chunk, owner, part or 0])

    def own_sends(chunk):
        push(chunk, r, None, row_of(other, y, core))
        push(chunk, r, None, row_of(x, up, core))
        push(chunk, r, None, row_of(x, down, core))
        push(chunk, r, None, sib)

    def step_a(chunk):
        o = row_of(other, y, core)
        got(chunk, o)
        push(chunk, o, None, row_of(x, up, core))
        push(chunk, o, None, row_of(x, down, core))
        push(chunk, o, None, sib)

    def step_b(chunk):
        o = row_of(x, down, core)
        got(chunk, o)
        push(chunk, o, 0, row_of(x, up, core))
        push(chunk, o, None, sib)
        o = row_of(x, up, core)
        got(chunk, o)
        push(chunk, o, 1, row_of(x, down, core))
        push(chunk, o, None, sib)

    def step_c(chunk):
        for yy in (down, up):
            o = row_of(other, yy, core)
            got(chunk, o)
            push(chunk, o, None, sib)

    def step_d(chunk):
        o = row_of(x, far, core)
        for part in range(2):
            got(chunk, o, part)
            push(chunk, o, part, row_of(other, y, core))
            push(chunk, o, part, sib)

    def step_e(chunk):
        o = row_of(other, far, core)
        for part in range(2):
            got(chunk, o, part)
            push(chunk, o, part, sib)

    def step_f(chunk):
        k = 1 - core
        for xx, yy in ((x, y), (other, y), (x, down), (x, up), (other, down), (other, up)):
            got(chunk, row_of(xx, yy, k))
        for xx in (x, other):
            for part in range(2):
                got(chunk, row_of(xx, far, k), part)

    def forward_piece(i):
        rows = pl.ds(i * 512, 512)
        v = jnp.dot(adj[rows, :], proj[...], preferred_element_type=F32)
        inb[0, rows, :] = v[:, :HALF]
        inb[1, rows, :] = v[:, HALF:]

    def history_and_scatter(h):
        sums[0] = jnp.zeros((BLK, HALF), F32)

        def pull(k, carry):
            block = hist[h][owner_ref[k] * 8 + slot_ref[k]]
            term = jnp.dot(tiles[k], block, preferred_element_type=F32)
            sums[k + 1] = term + sums[chain_ref[k]]
            return carry

        lax.fori_loop(0, K, pull, 0)

        def place(j, carry):
            v = inb[h, pl.ds(pl.multiple_of(j * BLK, BLK), BLK), :] + sums[chain_ref[K + j]]
            rs_snd[h, j // 2, pl.ds(pl.multiple_of((j % 2) * BLK, BLK), BLK), :] = v.astype(BF16)
            return carry

        lax.fori_loop(0, 2 * NC, place, 0)
        for d in range(1, NC):
            cc = (c + d) % NC
            send(rs_snd.at[h, cc], rs_rcv.at[h, c], rs_sem.at[h, c], r, cc)

    def activate(h):
        cols = pl.ds(h * HALF, HALF)
        mixed = rs_snd[h, c].astype(F32)
        for d in range(1, NC):
            cc = (c + d) % NC
            arrive(rs_rcv.at[h, cc], rs_sem.at[h, cc])
            mixed = mixed + rs_rcv[h, cc].astype(F32)
        s = 1.0 / (1.0 + jnp.exp(-mixed))
        act_ref[:, cols] = (mixed * s).astype(BF16)
        g = cot[:, cols].astype(F32) * s * (1.0 + mixed * (1.0 - s))
        gt[h, c] = g.T.astype(BF16)
        for d in range(1, NC):
            send(gt.at[h, c], gt.at[h, c], g_sem.at[h, c], r, (c + d) % NC)

    def backward(h):
        for d in range(NC):
            cc = (c + d) % NC
            if d:
                arrive(gt.at[h, cc], g_sem.at[h, cc])
            rows = pl.ds(pl.multiple_of(cc * SPAN, SPAN), SPAN)
            lhs = gt[h, cc]

            def tile(n, carry, rows=rows, lhs=lhs, d=d):
                cols = pl.ds(pl.multiple_of(n * 512, 512), 512)
                v = jnp.dot(lhs, adj[rows, cols], preferred_element_type=F32)
                out_t[:, cols] = v if d == 0 else out_t[:, cols] + v
                return carry

            lax.fori_loop(0, 8, tile, 0)

        def for_sib(q, carry):
            cols = pl.ds(pl.multiple_of((2 * q + 1 - core) * SPAN, SPAN), SPAN)
            sib_snd[h, q] = out_t[:, cols].astype(BF16)
            return carry

        lax.fori_loop(0, 8, for_sib, 0)
        send(sib_snd.at[h], sib_rcv.at[h], sib_sem.at[h], sib, c)

        def weight_term(o, total):
            cols = pl.ds(pl.multiple_of(o * SPAN, SPAN), SPAN)
            return total + jnp.dot(
                out_t[:, cols].astype(BF16), nodes_all[o], preferred_element_type=F32
            )

        gwt[pl.ds(h * HALF, HALF), :] = lax.fori_loop(
            0, NR, weight_term, jnp.zeros((HALF, HID), F32)
        )

    def scatter_rows(h):
        arrive(sib_rcv.at[h], sib_sem.at[h])

        def add(q, carry):
            cols = pl.ds(pl.multiple_of((2 * q + core) * SPAN, SPAN), SPAN)
            d_snd[h, q] = (out_t[:, cols] + sib_rcv[h, q].astype(F32)).astype(BF16)
            return carry

        lax.fori_loop(0, 8, add, 0)
        for d in range(1, 8):
            qq = (chip + d) % 8
            send(d_snd.at[h, qq], d_rcv.at[h, chip], d_sem.at[h, chip], qq * 2 + core, c)

    def collect_rows(h):
        total = d_snd[h, chip].astype(F32)
        for d in range(1, 8):
            qq = (chip + d) % 8
            arrive(d_rcv.at[h, qq], d_sem.at[h, qq])
            total = total + d_rcv[h, qq].astype(F32)
        return lax.dot_general(
            total.T.astype(BF16), w[:, pl.ds(h * HALF, HALF)], (((1,), (1,)), ((), ())),
            preferred_element_type=F32,
        )

    own_nodes.wait()
    own_sends(0)
    own_hist[0].wait()
    own_sends(1)
    own_hist[1].wait()
    for step in (step_a, step_b, step_c, step_d, step_e, step_f):
        step(0)
    step_a(1)
    w_copy.wait()

    def project(o, carry):
        rows = pl.ds(pl.multiple_of(o * SPAN, SPAN), SPAN)
        proj[rows, :] = jnp.dot(nodes_all[o], w[...], preferred_element_type=F32).astype(BF16)
        return carry

    lax.fori_loop(0, NR, project, 0)
    step_b(1)
    own_sends(2)
    adj_copy.wait()
    forward_piece(0)
    forward_piece(1)
    step_c(1)
    forward_piece(2)
    step_d(1)
    forward_piece(3)
    step_a(2)
    step_e(1)
    tiles_copy.wait()
    cot_copy.wait()
    step_f(1)
    history_and_scatter(0)
    for step in (step_b, step_c, step_d, step_e):
        step(2)
    activate(0)
    step_f(2)
    history_and_scatter(1)
    backward(0)
    scatter_rows(0)
    activate(1)
    backward(1)
    for d in range(1, NR):
        rr = (r + d) % NR
        send(
            gwt.at[pl.ds(pl.multiple_of(rr * 16, 16), 16)], gw_rcv1.at[r], gw1_sem.at[r], rr, c
        )
    scatter_rows(1)
    part = collect_rows(0)
    total = gwt[pl.ds(pl.multiple_of(r * 16, 16), 16), :]
    for d in range(1, NR):
        rr = (r + d) % NR
        arrive(gw_rcv1.at[rr], gw1_sem.at[rr])
        total = total + gw_rcv1[rr]
    gw_rcv2[c] = total
    for d in range(1, NC):
        send(gw_rcv2.at[c], gw_rcv2.at[c], gw2_sem.at[c], r, (c + d) % NC)
    for d in range(1, NC):
        cc = (c + d) % NC
        arrive(gw_rcv2.at[cc], gw2_sem.at[cc])
    total = gw_rcv2[0]
    for i in range(1, NC):
        total = total + gw_rcv2[i]
    gw_all[r] = total
    for d in range(1, NR):
        send(gw_all.at[r], gw_all.at[r], gw3_sem.at[r], (r + d) % NR, c)
    gn_ref[...] = (part + collect_rows(1)).astype(BF16)
    for d in range(1, NR):
        rr = (r + d) % NR
        arrive(gw_all.at[rr], gw3_sem.at[rr])
    gw_ref[...] = gw_all[...]
    for copy in sent:
        copy.wait_send()


def local(
    nodes, weight, adjacency, history, pull_owner, pull_slot, pull_target, hist_tiles, cotangent
):
    ask = jnp.concatenate([pull_target, jnp.arange(2 * NC, dtype=jnp.int32)])
    limit = jnp.minimum(jnp.arange(K + 2 * NC, dtype=jnp.int32), K)
    pulls = jnp.arange(K, dtype=jnp.int32)
    match = (pull_target[None, :] == ask[:, None]) & (pulls[None, :] < limit[:, None])
    chain = jnp.max(jnp.where(match, pulls[None, :] + 1, 0), axis=1)
    smem = pl.BlockSpec(memory_space=pltpu.SMEM)
    any_ = pl.BlockSpec(memory_space=pl.ANY)
    vmem = pl.BlockSpec(memory_space=pltpu.VMEM)
    dma = pltpu.SemaphoreType.DMA
    act, grad_nodes, gw = pl.pallas_call(
        kernel,
        out_shape=(
            jax.ShapeDtypeStruct((SPAN, HID), BF16),
            jax.ShapeDtypeStruct((SPAN, HID), BF16),
            jax.ShapeDtypeStruct((NR, 16, HID), F32),
        ),
        in_specs=[smem] * 3 + [any_] * 6,
        out_specs=(vmem,) * 3,
        scratch_shapes=[
            pltpu.VMEM((NR, SPAN, HID), BF16),
            pltpu.VMEM((128, BLK, HALF), BF16),
            pltpu.VMEM((128, BLK, HALF), BF16),
            pltpu.VMEM((2048, 4096), BF16),
            pltpu.VMEM((HID, HID), BF16),
            pltpu.VMEM((SPAN, HID), BF16),
            pltpu.VMEM((K, BLK, BLK), BF16),
            pltpu.VMEM((4096, HID), BF16),
            pltpu.VMEM((2, 2048, HALF), F32),
            pltpu.VMEM((K + 1, BLK, HALF), F32),
            pltpu.VMEM((2, NC, SPAN, HALF), BF16),
            pltpu.VMEM((2, NC, SPAN, HALF), BF16),
            pltpu.VMEM((2, NC, HALF, SPAN), BF16),
            pltpu.VMEM((HALF, 4096), F32),
            pltpu.VMEM((2, 8, HALF, SPAN), BF16),
            pltpu.VMEM((2, 8, HALF, SPAN), BF16),
            pltpu.VMEM((2, 8, HALF, SPAN), BF16),
            pltpu.VMEM((2, 8, HALF, SPAN), BF16),
            pltpu.VMEM((HID, HID), F32),
            pltpu.VMEM((NR, 16, HID), F32),
            pltpu.VMEM((16, HID), F32),
            pltpu.VMEM((NC, 16, HID), F32),
            pltpu.VMEM((NR, 16, HID), F32),
            dma((8,)),
            dma((160,)),
            dma((3, NR, 2)),
            dma((2, NC)),
            dma((2, NC)),
            dma((2,)),
            dma((2, 8)),
            dma((NR,)),
            dma((NC,)),
            dma((NR,)),
        ],
        compiler_params=pltpu.CompilerParams(
            collective_id=0, has_side_effects=True, vmem_limit_bytes=60 * 2**20
        ),
    )(
        chain, pull_owner[:, 0], pull_slot, nodes, weight, adjacency,
        history.reshape(8, BLK, HID), hist_tiles, cotangent,
    )
    all_nodes = nodes.shape[0] * NR * NC
    grad_weight = gw.reshape(HID, HID).T * (1.0 / math.sqrt(all_nodes))
    return act, grad_nodes, grad_weight


def solution(mesh):
    return jax.shard_map(
        local,
        mesh=mesh,
        in_specs=(
            P(("row", "col"), None),
            P(),
            P("row", "col"),
            P(("row", "col"), None),
            P(("row", "col"), None),
            P(("row", "col")),
            P(("row", "col")),
            P(("row", "col"), None, None),
            P(("row", "col"), None),
        ),
        out_specs=(P(("row", "col"), None), P(("row", "col"), None), P()),
        check_vma=False,
    )
```

```python
import math

import jax
import jax.numpy as jnp
from jax import lax
from jax.experimental import pallas as pl
from jax.experimental.pallas import tpu as pltpu
from jax.sharding import PartitionSpec as P

HID = 256
BLK = 128
HALF = 128
NR = 16
NC = 8
SPAN = 256
K = 32
MESH = pl.DeviceIdType.MESH
F32 = jnp.float32
BF16 = jnp.bfloat16


def kernel(
    owner_ref, slot_ref, target_ref, nodes_hbm, w_hbm, adj_hbm, hist_hbm, tiles_hbm, cot_hbm,
    act_ref, gn_ref, gw_ref,
    nodes_all, hist0, hist1, adj, w, cot, tiles, mix, inb, sums,
    rs_snd, rs_rcv, gt, sib_snd, sib_rcv, d_snd, d_rcv,
    gwt, gw_rcv1, gw_rcv2, gw_all, chain_v, chain_ref,
    loc_sem, snd_sem, ag_sem, rs_sem, g_sem, sib_snd_sem, sib_sem, d_snd_sem, d_sem,
    gw1_sem, gw2_sem, gw3_sem, near_sem, far_sem,
):
    r = lax.axis_index("row")
    c = lax.axis_index("col")
    core = r % 2
    chip = r // 2
    x = chip // 4
    y = chip % 4
    other = 1 - x
    up = (y + 1) % 4
    down = (y + 3) % 4
    far = (y + 2) % 4
    sib = r + 1 - 2 * core
    z = c % 4
    z_up = c - z + (z + 1) % 4
    z_down = c - z + (z + 3) % 4
    c_across = (c + 4) % NC

    def row_of(xx, yy, kk):
        return (xx * 4 + yy) * 2 + kk

    hist = (hist0, hist1)
    sent = []

    def send(src, dst, rsem, row, col):
        copy = pltpu.make_async_remote_copy(
            src_ref=src, dst_ref=dst, send_sem=snd_sem.at[len(sent)], recv_sem=rsem,
            device_id=(row, col), device_id_type=MESH,
        )
        copy.start()
        sent.append(copy)

    def arrive(dst, rsem):
        pltpu.make_async_remote_copy(
            src_ref=dst, dst_ref=dst, send_sem=snd_sem.at[0], recv_sem=rsem,
            device_id=(sib, c), device_id_type=MESH,
        ).wait_recv()

    def local(src, dst, i):
        copy = pltpu.make_async_copy(src, dst, loc_sem.at[i])
        copy.start()
        return copy

    def span(i):
        return pl.ds(pl.multiple_of(i * SPAN, SPAN), SPAN)

    own_nodes = local(nodes_hbm, nodes_all.at[span(r)], 0)
    own_hist = [
        local(hist_hbm.at[:, :, pl.ds(h * HALF, HALF)], hist[h].at[pl.ds(r * 8, 8)], 1 + h)
        for h in range(2)
    ]
    w_copy = local(w_hbm, w, 3)
    adj_copy = local(adj_hbm, adj, 4)
    tiles_copy = local(tiles_hbm, tiles, 5)
    cot_copy = local(cot_hbm, cot, 6)

    barrier = pltpu.get_barrier_semaphore()
    for rr, cc in (
        (row_of(other, y, core), c), (row_of(x, up, core), c), (row_of(x, down, core), c), (sib, c),
        (r, z_up), (r, z_down), (r, c_across),
    ):
        pl.semaphore_signal(barrier, inc=1, device_id=(rr, cc), device_id_type=MESH)
    pl.semaphore_wait(barrier, 7)

    def piece(chunk, owner, part):
        if chunk == 0:
            if part is None:
                return nodes_all.at[span(owner)]
            return nodes_all.at[pl.ds(pl.multiple_of(owner * SPAN + part * 128, 128), 128)]
        if part is None:
            return hist[chunk - 1].at[pl.ds(owner * 8, 8)]
        return hist[chunk - 1].at[pl.ds(owner * 8 + part * 4, 4)]

    def push(chunk, owner, part, dest):
        ref = piece(chunk, owner, part)
        send(ref, ref, ag_sem.at[chunk, owner, part or 0], dest, c)

    def got(chunk, owner, part=None):
        arrive(piece(chunk, owner, part), ag_sem.at[chunk, owner, part or 0])

    def own_y(chunk):
        push(chunk, r, None, row_of(x, up, core))
        push(chunk, r, None, row_of(x, down, core))

    def own_x(chunk):
        push(chunk, r, None, row_of(other, y, core))
        push(chunk, r, None, sib)

    def step_a(chunk):
        o = row_of(other, y, core)
        got(chunk, o)
        push(chunk, o, None, row_of(x, up, core))
        push(chunk, o, None, row_of(x, down, core))
        push(chunk, o, None, sib)

    def step_b(chunk):
        o = row_of(x, down, core)
        got(chunk, o)
        push(chunk, o, 0, row_of(x, up, core))
        push(chunk, o, None, sib)
        o = row_of(x, up, core)
        got(chunk, o)
        push(chunk, o, 1, row_of(x, down, core))
        push(chunk, o, None, sib)

    def step_c(chunk):
        for yy in (down, up):
            o = row_of(other, yy, core)
            got(chunk, o)
            push(chunk, o, None, sib)

    def step_d(chunk):
        o = row_of(x, far, core)
        for part in range(2):
            got(chunk, o, part)
            push(chunk, o, part, row_of(other, y, core))
            push(chunk, o, part, sib)

    def step_e(chunk):
        o = row_of(other, far, core)
        for part in range(2):
            got(chunk, o, part)
            push(chunk, o, part, sib)

    def step_f(chunk):
        k = 1 - core
        for xx, yy in ((x, y), (other, y), (x, down), (x, up), (other, down), (other, up)):
            got(chunk, row_of(xx, yy, k))
        for xx in (x, other):
            for part in range(2):
                got(chunk, row_of(xx, far, k), part)

    def make_chain():
        lane = lax.broadcasted_iota(jnp.int32, (K, 128), 1)
        sub = lax.broadcasted_iota(jnp.int32, (K, 128), 0)
        ask, mine = lane - K, sub
        for k in range(K):
            t = target_ref[k]
            ask = jnp.where(lane == k, t, ask)
            mine = jnp.where(sub == k, t, mine)
        match = (mine == ask) & (sub < jnp.minimum(lane, K))
        chain_v[...] = jnp.max(jnp.where(match, sub + 1, 0), axis=0, keepdims=True)
        return local(chain_v, chain_ref, 7)

    def forward_piece(i):
        rows = pl.ds(i * 512, 512)
        m = jnp.dot(adj[rows, :], nodes_all[...], preferred_element_type=F32).astype(BF16)
        mix[rows, :] = m
        v = jnp.dot(m, w[...], preferred_element_type=F32)
        inb[0, rows, :] = v[:, :HALF]
        inb[1, rows, :] = v[:, HALF:]

    def history_and_scatter(h):
        sums[0] = jnp.zeros((BLK, HALF), F32)

        def product(k, carry):
            block = hist[h][owner_ref[k] * 8 + slot_ref[k]]
            sums[k + 1] = jnp.dot(tiles[k], block, preferred_element_type=F32)
            return carry

        lax.fori_loop(0, K, product, 0, unroll=8)

        def link(k, carry):
            sums[k + 1] = sums[k + 1] + sums[chain_ref[0, k]]
            return carry

        lax.fori_loop(0, K, link, 0, unroll=4)
        for d in range(1, NC + 1):
            cc = (c + d) % NC
            for i in range(2):
                j = cc * 2 + i
                v = inb[h, pl.ds(pl.multiple_of(j * BLK, BLK), BLK), :] + sums[chain_ref[0, K + j]]
                rs_snd[h, cc, pl.ds(i * BLK, BLK), :] = v.astype(BF16)
            if d < NC:
                send(rs_snd.at[h, cc], rs_rcv.at[h, c], rs_sem.at[h, c], r, cc)

    def activate(h):
        cols = pl.ds(h * HALF, HALF)
        mixed = rs_snd[h, c].astype(F32)
        for d in range(1, NC):
            cc = (c + NC - d) % NC
            arrive(rs_rcv.at[h, cc], rs_sem.at[h, cc])
            mixed = mixed + rs_rcv[h, cc].astype(F32)
        s = 1.0 / (1.0 + jnp.exp(-mixed))
        g = cot[:, cols].astype(F32) * s * (1.0 + mixed * (1.0 - s))
        own = gt.at[h, :, span(c)]
        own[...] = g.T.astype(BF16)
        for d in range(1, NC):
            send(own, own, g_sem.at[h, c], r, (c + d) % NC)
        act_ref[:, cols] = (mixed * s).astype(BF16)

    def sib_copy(h, q):
        return pltpu.make_async_remote_copy(
            src_ref=sib_snd.at[h, q], dst_ref=sib_rcv.at[h, q], send_sem=sib_snd_sem.at[h, q],
            recv_sem=sib_sem.at[h, q], device_id=(sib, c), device_id_type=MESH,
        )

    def row_copy(h, q):
        return pltpu.make_async_remote_copy(
            src_ref=d_snd.at[h, q], dst_ref=d_rcv.at[h, chip], send_sem=d_snd_sem.at[h, q],
            recv_sem=d_sem.at[h, chip], device_id=(q * 2 + core, c), device_id_type=MESH,
        )

    def backward(h):
        for d in range(1, NC):
            cc = (c + NC - d) % NC
            arrive(gt.at[h, :, span(cc)], g_sem.at[h, cc])
        gwt[pl.ds(h * HALF, HALF), :] = jnp.dot(gt[h], mix[...], preferred_element_type=F32)
        if h:
            for d in range(1, NR):
                rr = (r + d) % NR
                rows = pl.ds(pl.multiple_of(rr * 16, 16), 16)
                send(gwt.at[rows], gw_rcv1.at[r], gw1_sem.at[r], rr, c)

        def for_sib(d, carry):
            q = (chip + d) % 8
            v = jnp.dot(gt[h], adj[:, span(2 * q + 1 - core)], preferred_element_type=F32)
            sib_snd[h, q] = v.astype(BF16)
            sib_copy(h, q).start()
            return carry

        lax.fori_loop(1, 9, for_sib, 0)

        def summed(q):
            v = jnp.dot(gt[h], adj[:, span(2 * q + core)], preferred_element_type=F32)
            arrive(sib_rcv.at[h, q], sib_sem.at[h, q])
            d_snd[h, q] = (v + sib_rcv[h, q].astype(F32)).astype(BF16)

        def for_chip(d, carry):
            q = (chip + d) % 8
            summed(q)
            row_copy(h, q).start()
            return carry

        lax.fori_loop(1, 8, for_chip, 0)
        summed(chip)

    def collect_rows(h):
        total = d_snd[h, chip].astype(F32)
        for d in range(1, 8):
            qq = (chip + 8 - d) % 8
            arrive(d_rcv.at[h, qq], d_sem.at[h, qq])
            total = total + d_rcv[h, qq].astype(F32)
        return lax.dot_general(
            total.T.astype(BF16), w[:, pl.ds(h * HALF, HALF)], (((1,), (1,)), ((), ())),
            preferred_element_type=F32,
        )

    own_nodes.wait()
    own_y(0)
    own_x(0)
    own_hist[0].wait()
    own_y(1)
    own_x(1)
    for cc in (z_up, z_down):
        pl.semaphore_signal(near_sem, inc=1, device_id=(r, cc), device_id_type=MESH)
    own_hist[1].wait()
    chain_copy = make_chain()
    step_b(0)
    step_a(0)
    own_x(2)
    pl.semaphore_wait(near_sem, 2)
    pl.semaphore_signal(far_sem, inc=1, device_id=(r, c_across), device_id_type=MESH)
    step_c(0)
    step_d(0)
    step_b(1)
    own_y(2)
    step_a(1)
    step_e(0)
    step_f(0)
    w_copy.wait()
    adj_copy.wait()
    forward_piece(0)
    forward_piece(1)
    step_d(1)
    forward_piece(2)
    forward_piece(3)
    step_b(2)
    step_a(2)
    step_e(1)
    step_c(1)
    tiles_copy.wait()
    cot_copy.wait()
    chain_copy.wait()
    pl.semaphore_wait(far_sem, 1)
    step_f(1)
    history_and_scatter(0)
    step_d(2)
    step_c(2)
    activate(0)
    step_e(2)
    step_f(2)
    history_and_scatter(1)
    backward(0)
    activate(1)
    part = collect_rows(0)
    backward(1)
    total = gwt[pl.ds(pl.multiple_of(r * 16, 16), 16), :]
    for d in range(1, NR):
        rr = (r + NR - d) % NR
        arrive(gw_rcv1.at[rr], gw1_sem.at[rr])
        total = total + gw_rcv1[rr]
    gw_rcv2[c] = total
    for d in range(1, NC):
        send(gw_rcv2.at[c], gw_rcv2.at[c], gw2_sem.at[c], r, (c + d) % NC)
    for d in range(1, NC):
        cc = (c + NC - d) % NC
        arrive(gw_rcv2.at[cc], gw2_sem.at[cc])
    total = gw_rcv2[0]
    for i in range(1, NC):
        total = total + gw_rcv2[i]
    gw_all[r] = total
    for d in range(1, NR):
        send(gw_all.at[r], gw_all.at[r], gw3_sem.at[r], (r + d) % NR, c)
    gn_ref[...] = (part + collect_rows(1)).astype(BF16)
    for d in range(1, NR):
        rr = (r + NR - d) % NR
        arrive(gw_all.at[rr], gw3_sem.at[rr])
    gw_ref[...] = gw_all[...]
    for copy in sent:
        copy.wait_send()

    def sent_tiles(d, carry):
        q = (chip + d) % 8
        for h in range(2):
            sib_copy(h, q).wait_send()
            row_copy(h, q).wait_send()
        return carry

    lax.fori_loop(1, 8, sent_tiles, 0)
    for h in range(2):
        sib_copy(h, chip).wait_send()


def finish(scale, act_ref, gn_ref, gw_ref, act_out, gn_out, gw_out, sem):
    copies = [
        pltpu.make_async_copy(act_ref, act_out, sem.at[0]),
        pltpu.make_async_copy(gn_ref, gn_out, sem.at[1]),
    ]
    for copy in copies:
        copy.start()
    gw_out[...] = gw_ref[...].T * scale
    for copy in copies:
        copy.wait()


def local(
    nodes, weight, adjacency, history, pull_owner, pull_slot, pull_target, hist_tiles, cotangent
):
    smem = pl.BlockSpec(memory_space=pltpu.SMEM)
    any_ = pl.BlockSpec(memory_space=pl.ANY)
    vmem = pl.BlockSpec(memory_space=pltpu.VMEM)
    dma = pltpu.SemaphoreType.DMA
    act, grad_nodes, gw = pl.pallas_call(
        kernel,
        out_shape=(
            jax.ShapeDtypeStruct((SPAN, HID), BF16),
            jax.ShapeDtypeStruct((SPAN, HID), BF16),
            jax.ShapeDtypeStruct((NR, 16, HID), F32),
        ),
        in_specs=[smem] * 3 + [any_] * 6,
        out_specs=(vmem,) * 3,
        scratch_shapes=[
            pltpu.VMEM((4096, HID), BF16),
            pltpu.VMEM((128, BLK, HALF), BF16),
            pltpu.VMEM((128, BLK, HALF), BF16),
            pltpu.VMEM((2048, 4096), BF16),
            pltpu.VMEM((HID, HID), BF16),
            pltpu.VMEM((SPAN, HID), BF16),
            pltpu.VMEM((K, BLK, BLK), BF16),
            pltpu.VMEM((2048, HID), BF16),
            pltpu.VMEM((2, 2048, HALF), F32),
            pltpu.VMEM((K + 1, BLK, HALF), F32),
            pltpu.VMEM((2, NC, SPAN, HALF), BF16),
            pltpu.VMEM((2, NC, SPAN, HALF), BF16),
            pltpu.VMEM((2, HALF, 2048), BF16),
            pltpu.VMEM((2, 8, HALF, SPAN), BF16),
            pltpu.VMEM((2, 8, HALF, SPAN), BF16),
            pltpu.VMEM((2, 8, HALF, SPAN), BF16),
            pltpu.VMEM((2, 8, HALF, SPAN), BF16),
            pltpu.VMEM((HID, HID), F32),
            pltpu.VMEM((NR, 16, HID), F32),
            pltpu.VMEM((NC, 16, HID), F32),
            pltpu.VMEM((NR, 16, HID), F32),
            pltpu.VMEM((1, 128), jnp.int32),
            pltpu.SMEM((1, 128), jnp.int32),
            dma((8,)),
            dma((160,)),
            dma((3, NR, 2)),
            dma((2, NC)),
            dma((2, NC)),
            dma((2, 8)),
            dma((2, 8)),
            dma((2, 8)),
            dma((2, 8)),
            dma((NR,)),
            dma((NC,)),
            dma((NR,)),
            pltpu.SemaphoreType.REGULAR,
            pltpu.SemaphoreType.REGULAR,
        ],
        compiler_params=pltpu.CompilerParams(
            collective_id=0, has_side_effects=True, vmem_limit_bytes=60 * 2**20
        ),
    )(
        pull_owner[:, 0], pull_slot, pull_target, nodes, weight, adjacency,
        history.reshape(8, BLK, HID), hist_tiles, cotangent,
    )
    all_nodes = nodes.shape[0] * NR * NC
    return pl.pallas_call(
        lambda *refs: finish(1.0 / math.sqrt(all_nodes), *refs),
        out_shape=(
            jax.ShapeDtypeStruct((SPAN, HID), BF16),
            jax.ShapeDtypeStruct((SPAN, HID), BF16),
            jax.ShapeDtypeStruct((HID, HID), F32),
        ),
        in_specs=[any_, any_, vmem],
        out_specs=(any_, any_, vmem),
        scratch_shapes=[dma((2,))],
    )(act, grad_nodes, gw.reshape(HID, HID))


def solution(mesh):
    return jax.shard_map(
        local,
        mesh=mesh,
        in_specs=(
            P(("row", "col"), None),
            P(),
            P("row", "col"),
            P(("row", "col"), None),
            P(("row", "col"), None),
            P(("row", "col")),
            P(("row", "col")),
            P(("row", "col"), None, None),
            P(("row", "col"), None),
        ),
        out_specs=(P(("row", "col"), None), P(("row", "col"), None), P()),
        check_vma=False,
    )
```

```python
import math

import jax
import jax.numpy as jnp
from jax import lax
from jax.experimental import pallas as pl
from jax.experimental.pallas import tpu as pltpu
from jax.sharding import PartitionSpec as P

HID = 256
BLK = 128
HALF = 128
NR = 16
NC = 8
SPAN = 256
K = 32
MESH = pl.DeviceIdType.MESH
F32 = jnp.float32
BF16 = jnp.bfloat16


def kernel(
    owner_hbm, slot_hbm, target_hbm, nodes_hbm, w_hbm, adj_hbm, hist_hbm, tiles_hbm, cot_hbm,
    act_hbm, gn_hbm, gw_hbm,
    owner_ref, slot_ref, target_ref, act_ref, gn_ref,
    nodes_all, hist0, hist1, adj, w, cot, tiles, mix, mix_rcv, mix_snd, mix_far, mix_own, sums,
    rs_snd, rs_rcv, gt, sib_snd, sib_rcv, d_snd, d_rcv,
    gwt, gw_rcv1, gw_rcv2, gw_all, chain_v, chain_ref,
    loc_sem, snd_sem, ag_sem, rs_sem, g_sem, sib_sem, d_sem, one_sem, near_sem, far_sem,
):
    r = lax.axis_index("row")
    c = lax.axis_index("col")
    core = r % 2
    chip = r // 2
    x = chip // 4
    y = chip % 4
    other = 1 - x
    up = (y + 1) % 4
    down = (y + 3) % 4
    far = (y + 2) % 4
    sib = r + 1 - 2 * core
    z = c % 4
    z_up = c - z + (z + 1) % 4
    z_down = c - z + (z + 3) % 4
    c_across = (c + 4) % NC

    def row_of(xx, yy, kk):
        return (xx * 4 + yy) * 2 + kk

    hist = (hist0, hist1)
    groups = dict(mixz=3, mixx=15, rs0=4, rs1=5, g0=6, g1=7, sib0=8, sib1=9, d0=10, d1=11, w1=12, w2=13, w3=14)
    col_order = [
        ((c // 4 + dx) % 2) * 4 + (z + dz) % 4
        for dx, dz in ((1, 2), (0, 2), (1, 1), (0, 1), (1, 3), (0, 3), (1, 0))
    ]

    def copy_of(src, dst, group, rsem, row, col):
        return pltpu.make_async_remote_copy(
            src_ref=src, dst_ref=dst, send_sem=snd_sem.at[groups.get(group, group)], recv_sem=rsem,
            device_id=(row, col), device_id_type=MESH,
        )

    def send(src, dst, group, rsem, row, col):
        copy_of(src, dst, group, rsem, row, col).start()

    def arrive(dst, rsem):
        copy_of(dst, dst, 0, rsem, sib, c).wait_recv()

    def all_sent(src, group):
        copy_of(src, src, group, one_sem.at[0], sib, c).wait_send()

    def local(src, dst, i):
        copy = pltpu.make_async_copy(src, dst, loc_sem.at[i])
        copy.start()
        return copy

    def span(i):
        return pl.ds(pl.multiple_of(i * SPAN, SPAN), SPAN)

    own_nodes = local(nodes_hbm, nodes_all.at[span(r)], 0)
    own_hist = [
        local(hist_hbm.at[:, :, pl.ds(h * HALF, HALF)], hist[h].at[pl.ds(r * 8, 8)], 1 + h)
        for h in range(2)
    ]
    w_copy = local(w_hbm, w, 3)
    adj_copy = local(adj_hbm, adj, 4)
    tiles_copy = local(tiles_hbm, tiles, 5)
    cot_copy = local(cot_hbm, cot, 6)
    pull_copies = [
        local(src, dst, 8 + i)
        for i, (src, dst) in enumerate(
            ((target_hbm, target_ref), (owner_hbm, owner_ref), (slot_hbm, slot_ref))
        )
    ]

    barrier = pltpu.get_barrier_semaphore()
    for rr, cc in (
        (row_of(other, y, core), c), (row_of(x, up, core), c), (row_of(x, down, core), c), (sib, c),
        (r, z_up), (r, z_down), (r, c_across),
    ):
        pl.semaphore_signal(barrier, inc=1, device_id=(rr, cc), device_id_type=MESH)
    pl.semaphore_wait(barrier, 7)

    def piece(chunk, owner, part):
        if chunk == 0:
            if part is None:
                return nodes_all.at[span(owner)]
            return nodes_all.at[pl.ds(pl.multiple_of(owner * SPAN + part * 128, 128), 128)]
        if part is None:
            return hist[chunk - 1].at[pl.ds(owner * 8, 8)]
        return hist[chunk - 1].at[pl.ds(owner * 8 + part * 4, 4)]

    def push(chunk, owner, part, dest):
        ref = piece(chunk, owner, part)
        send(ref, ref, chunk, ag_sem.at[chunk, owner, part or 0], dest, c)

    def got(chunk, owner, part=None):
        arrive(piece(chunk, owner, part), ag_sem.at[chunk, owner, part or 0])

    def own_y(chunk):
        push(chunk, r, None, row_of(x, up, core))
        push(chunk, r, None, row_of(x, down, core))

    def own_x(chunk):
        push(chunk, r, None, row_of(other, y, core))
        push(chunk, r, None, sib)

    def step_a(chunk):
        o = row_of(other, y, core)
        got(chunk, o)
        push(chunk, o, None, row_of(x, up, core))
        push(chunk, o, None, row_of(x, down, core))
        push(chunk, o, None, sib)

    def step_b(chunk):
        o = row_of(x, down, core)
        got(chunk, o)
        push(chunk, o, 0, row_of(x, up, core))
        push(chunk, o, None, sib)
        o = row_of(x, up, core)
        got(chunk, o)
        push(chunk, o, 1, row_of(x, down, core))
        push(chunk, o, None, sib)

    def step_c(chunk):
        for yy in (down, up):
            o = row_of(other, yy, core)
            got(chunk, o)
            push(chunk, o, None, sib)

    def step_d(chunk):
        o = row_of(x, far, core)
        for part in range(2):
            got(chunk, o, part)
            push(chunk, o, part, row_of(other, y, core))
            push(chunk, o, part, sib)

    def step_e(chunk):
        o = row_of(other, far, core)
        for part in range(2):
            got(chunk, o, part)
            push(chunk, o, part, sib)

    def step_f(chunk):
        k = 1 - core
        for xx, yy in ((x, y), (other, y), (x, down), (x, up), (other, down), (other, up)):
            got(chunk, row_of(xx, yy, k))
        for xx in (x, other):
            for part in range(2):
                got(chunk, row_of(xx, far, k), part)

    def make_chain():
        lane = lax.broadcasted_iota(jnp.int32, (K, 128), 1)
        sub = lax.broadcasted_iota(jnp.int32, (K, 128), 0)
        ask, mine = lane - K, sub
        for k in range(K):
            t = target_ref[k]
            ask = jnp.where(lane == k, t, ask)
            mine = jnp.where(sub == k, t, mine)
        match = (mine == ask) & (sub < jnp.minimum(lane, K))
        chain_v[...] = jnp.max(jnp.where(match, sub + 1, 0), axis=0, keepdims=True)
        return local(chain_v, chain_ref, 7)

    def forward_piece(i):
        rows = pl.ds(i * 512, 512)
        mix[rows, :] = jnp.dot(
            adj[rows, :], nodes_all[...], preferred_element_type=F32
        ).astype(BF16)

    def scatter_mix():
        for dz in (2, 1, 3):
            zz = (z + dz) % 4
            for xx in range(2):
                send(
                    mix.at[span(xx * 4 + zz)], mix_rcv.at[z, xx], "mixz", one_sem.at[0],
                    r, c - z + zz,
                )

    def cross_mix():
        arrive(mix_rcv.at[pl.ds(0, 3)], one_sem.at[0])
        xx = c // 4
        theirs = mix[span((1 - xx) * 4 + z), :].astype(F32)
        for dz in range(1, 4):
            theirs = theirs + mix_rcv[(z + dz) % 4, 1 - xx].astype(F32)
        mix_snd[...] = theirs.astype(BF16)
        send(mix_snd, mix_far, "mixx", one_sem.at[4], r, c_across)

    def collect_mix():
        xx = c // 4
        total = mix[span(c), :].astype(F32)
        for dz in range(1, 4):
            total = total + mix_rcv[(z + dz) % 4, xx].astype(F32)
        arrive(mix_far, one_sem.at[4])
        mix_own[...] = (total + mix_far[...].astype(F32)).astype(BF16)

    def history_and_scatter(h):
        sums[0] = jnp.zeros((BLK, HALF), F32)

        def product(k, carry):
            block = hist[h][owner_ref[k] * 8 + slot_ref[k]]
            sums[k + 1] = jnp.dot(tiles[k], block, preferred_element_type=F32)
            return carry

        lax.fori_loop(0, K, product, 0, unroll=8)

        def link(k, carry):
            sums[k + 1] = sums[k + 1] + sums[chain_ref[0, k]]
            return carry

        lax.fori_loop(0, K, link, 0, unroll=4)
        for cc in col_order + [c]:
            for i in range(2):
                v = sums[chain_ref[0, K + cc * 2 + i]]
                rs_snd[h, cc, pl.ds(i * BLK, BLK), :] = v.astype(BF16)
            if cc is not c:
                send(rs_snd.at[h, cc], rs_rcv.at[h, c], f"rs{h}", rs_sem.at[h], r, cc)

    def activate(h):
        cols = pl.ds(h * HALF, HALF)
        mixed = jnp.dot(mix_own[...], w[:, cols], preferred_element_type=F32)
        mixed = mixed + rs_snd[h, c].astype(F32)
        arrive(rs_rcv.at[h, pl.ds(0, NC - 1)], rs_sem.at[h])
        for cc in col_order:
            mixed = mixed + rs_rcv[h, cc].astype(F32)
        s = 1.0 / (1.0 + jnp.exp(-mixed))
        g = cot[:, cols].astype(F32) * s * (1.0 + mixed * (1.0 - s))
        g = g.T.astype(BF16)
        own = gt.at[h, :, span(c)]
        own[...] = g
        for cc in col_order:
            send(own, own, f"g{h}", g_sem.at[h], r, cc)
        gwt[pl.ds(h * HALF, HALF), :] = jnp.dot(g, mix_own[...], preferred_element_type=F32)
        act_ref[:, cols] = (mixed * s).astype(BF16)

    def near(i):
        return ((x + 1 - i % 2) % 2) * 4 + (y + 3 - i // 2) % 4

    def sib_copy(h, q):
        return copy_of(sib_snd.at[h, q], sib_rcv.at[h, q], f"sib{h}", sib_sem.at[h, q], sib, c)

    def row_copy(h, q):
        return copy_of(
            d_snd.at[h, q], d_rcv.at[h, chip], f"d{h}", d_sem.at[h], q * 2 + core, c
        )

    def backward(h):
        arrive(gt.at[h, :, pl.ds(0, (NC - 1) * SPAN)], g_sem.at[h])

        def for_sib(i, carry):
            q = near(i)
            v = jnp.dot(gt[h], adj[:, span(2 * q + 1 - core)], preferred_element_type=F32)
            sib_snd[h, q] = v.astype(BF16)
            sib_copy(h, q).start()
            return carry

        lax.fori_loop(0, 8, for_sib, 0)

        def summed(q):
            v = jnp.dot(gt[h], adj[:, span(2 * q + core)], preferred_element_type=F32)
            arrive(sib_rcv.at[h, q], sib_sem.at[h, q])
            d_snd[h, q] = (v + sib_rcv[h, q].astype(F32)).astype(BF16)

        def for_chip(i, carry):
            q = near(i)
            summed(q)
            row_copy(h, q).start()
            return carry

        lax.fori_loop(0, 7, for_chip, 0)
        summed(chip)

    def collect_rows(h):
        arrive(d_rcv.at[h, pl.ds(0, 7)], d_sem.at[h])
        total = d_snd[h, chip].astype(F32)
        for d in range(1, 8):
            total = total + d_rcv[h, (chip + d) % 8].astype(F32)
        return lax.dot_general(
            total.T.astype(BF16), w[:, pl.ds(h * HALF, HALF)], (((1,), (1,)), ((), ())),
            preferred_element_type=F32,
        )

    def weight_rows(i):
        return pl.ds(pl.multiple_of(i * 16, 16), 16)

    own_nodes.wait()
    own_y(0)
    own_x(0)
    own_hist[0].wait()
    own_y(1)
    own_x(1)
    for cc in (z_up, z_down):
        pl.semaphore_signal(near_sem, inc=1, device_id=(r, cc), device_id_type=MESH)
    own_hist[1].wait()
    for copy in pull_copies:
        copy.wait()
    chain_copy = make_chain()
    step_b(0)
    step_a(0)
    own_x(2)
    pl.semaphore_wait(near_sem, 2)
    pl.semaphore_signal(far_sem, inc=1, device_id=(r, c_across), device_id_type=MESH)
    step_c(0)
    step_d(0)
    step_b(1)
    own_y(2)
    step_a(1)
    step_e(0)
    step_f(0)
    w_copy.wait()
    adj_copy.wait()
    forward_piece(0)
    forward_piece(1)
    step_d(1)
    forward_piece(2)
    forward_piece(3)
    pl.semaphore_wait(far_sem, 1)
    scatter_mix()
    step_b(2)
    step_a(2)
    step_e(1)
    step_c(1)
    tiles_copy.wait()
    cot_copy.wait()
    chain_copy.wait()
    step_f(1)
    history_and_scatter(0)
    step_d(2)
    step_c(2)
    cross_mix()
    step_e(2)
    step_f(2)
    history_and_scatter(1)
    collect_mix()
    activate(0)
    activate(1)
    act_copy = local(act_ref, act_hbm, 11)
    for d in range(1, NR):
        rr = (r + d) % NR
        send(gwt.at[weight_rows(rr)], gw_rcv1.at[r], "w1", one_sem.at[1], rr, c)
    backward(0)
    arrive(gw_rcv1.at[pl.ds(0, NR - 1)], one_sem.at[1])
    total = gwt[weight_rows(r), :]
    for d in range(1, NR):
        total = total + gw_rcv1[(r + d) % NR]
    gw_rcv2[c] = total
    for cc in col_order:
        send(gw_rcv2.at[c], gw_rcv2.at[c], "w2", one_sem.at[2], r, cc)
    backward(1)
    arrive(gw_rcv2.at[pl.ds(0, NC - 1)], one_sem.at[2])
    total = gw_rcv2[0]
    for i in range(1, NC):
        total = total + gw_rcv2[i]
    gw_all[r] = total
    for d in range(1, NR):
        send(gw_all.at[r], gw_all.at[r], "w3", one_sem.at[3], (r + d) % NR, c)
    part = collect_rows(0)
    gn_ref[...] = (part + collect_rows(1)).astype(BF16)
    gn_copy = local(gn_ref, gn_hbm, 12)
    arrive(gw_all.at[pl.ds(0, NR - 1)], one_sem.at[3])
    gw_copy = local(gw_all, gw_hbm, 13)
    all_sent(nodes_all.at[pl.ds(0, 15 * SPAN)], 0)
    for h in range(2):
        all_sent(hist[h].at[pl.ds(0, 120)], 1 + h)
        all_sent(rs_snd.at[h, pl.ds(0, NC - 1)], f"rs{h}")
        all_sent(gt.at[h, :, pl.ds(0, (NC - 1) * SPAN)], f"g{h}")
        all_sent(sib_snd.at[h], f"sib{h}")
        all_sent(d_snd.at[h, pl.ds(0, 7)], f"d{h}")
    all_sent(mix.at[pl.ds(0, 6 * SPAN)], "mixz")
    all_sent(mix_snd, "mixx")
    all_sent(gwt.at[pl.ds(0, (NR - 1) * 16)], "w1")
    all_sent(gw_rcv2.at[pl.ds(0, NC - 1)], "w2")
    all_sent(gw_all.at[pl.ds(0, NR - 1)], "w3")
    for copy in (act_copy, gn_copy, gw_copy):
        copy.wait()


def finish(scale, act_ref, gn_ref, gw_ref, act_out, gn_out, gw_out):
    act_out[...] = act_ref[...]
    gn_out[...] = gn_ref[...]
    gw_out[...] = gw_ref[...].T * scale


def local(
    nodes, weight, adjacency, history, pull_owner, pull_slot, pull_target, hist_tiles, cotangent
):
    any_ = pl.BlockSpec(memory_space=pl.ANY)
    vmem = pl.BlockSpec(memory_space=pltpu.VMEM)
    dma = pltpu.SemaphoreType.DMA
    act, grad_nodes, gw = pl.pallas_call(
        kernel,
        out_shape=(
            jax.ShapeDtypeStruct((SPAN, HID), BF16),
            jax.ShapeDtypeStruct((SPAN, HID), BF16),
            jax.ShapeDtypeStruct((NR, 16, HID), F32),
        ),
        in_specs=[any_] * 9,
        out_specs=(any_,) * 3,
        scratch_shapes=[
            pltpu.SMEM((K,), jnp.int32),
            pltpu.SMEM((K,), jnp.int32),
            pltpu.SMEM((K,), jnp.int32),
            pltpu.VMEM((SPAN, HID), BF16),
            pltpu.VMEM((SPAN, HID), BF16),
            pltpu.VMEM((4096, HID), BF16),
            pltpu.VMEM((128, BLK, HALF), BF16),
            pltpu.VMEM((128, BLK, HALF), BF16),
            pltpu.VMEM((2048, 4096), BF16),
            pltpu.VMEM((HID, HID), BF16),
            pltpu.VMEM((SPAN, HID), BF16),
            pltpu.VMEM((K, BLK, BLK), BF16),
            pltpu.VMEM((2048, HID), BF16),
            pltpu.VMEM((4, 2, SPAN, HID), BF16),
            pltpu.VMEM((SPAN, HID), BF16),
            pltpu.VMEM((SPAN, HID), BF16),
            pltpu.VMEM((SPAN, HID), BF16),
            pltpu.VMEM((K + 1, BLK, HALF), F32),
            pltpu.VMEM((2, NC, SPAN, HALF), BF16),
            pltpu.VMEM((2, NC, SPAN, HALF), BF16),
            pltpu.VMEM((2, HALF, 2048), BF16),
            pltpu.VMEM((2, 8, HALF, SPAN), BF16),
            pltpu.VMEM((2, 8, HALF, SPAN), BF16),
            pltpu.VMEM((2, 8, HALF, SPAN), BF16),
            pltpu.VMEM((2, 8, HALF, SPAN), BF16),
            pltpu.VMEM((HID, HID), F32),
            pltpu.VMEM((NR, 16, HID), F32),
            pltpu.VMEM((NC, 16, HID), F32),
            pltpu.VMEM((NR, 16, HID), F32),
            pltpu.VMEM((1, 128), jnp.int32),
            pltpu.SMEM((1, 128), jnp.int32),
            dma((14,)),
            dma((16,)),
            dma((3, NR, 2)),
            dma((2,)),
            dma((2,)),
            dma((2, 8)),
            dma((2,)),
            dma((5,)),
            pltpu.SemaphoreType.REGULAR,
            pltpu.SemaphoreType.REGULAR,
        ],
        compiler_params=pltpu.CompilerParams(
            collective_id=0, has_side_effects=True, vmem_limit_bytes=60 * 2**20
        ),
    )(
        pull_owner[:, 0], pull_slot, pull_target, nodes, weight, adjacency,
        history.reshape(8, BLK, HID), hist_tiles, cotangent,
    )
    all_nodes = nodes.shape[0] * NR * NC
    return pl.pallas_call(
        lambda *refs: finish(1.0 / math.sqrt(all_nodes), *refs),
        out_shape=(
            jax.ShapeDtypeStruct((SPAN, HID), BF16),
            jax.ShapeDtypeStruct((SPAN, HID), BF16),
            jax.ShapeDtypeStruct((HID, HID), F32),
        ),
        in_specs=[vmem] * 3,
        out_specs=(vmem,) * 3,
    )(act, grad_nodes, gw.reshape(HID, HID))


def solution(mesh):
    return jax.shard_map(
        local,
        mesh=mesh,
        in_specs=(
            P(("row", "col"), None),
            P(),
            P("row", "col"),
            P(("row", "col"), None),
            P(("row", "col"), None),
            P(("row", "col")),
            P(("row", "col")),
            P(("row", "col"), None, None),
            P(("row", "col"), None),
        ),
        out_specs=(P(("row", "col"), None), P(("row", "col"), None), P()),
        check_vma=False,
    )
```

```python
import math

import jax
import jax.numpy as jnp
from jax import lax
from jax.experimental import pallas as pl
from jax.experimental.pallas import tpu as pltpu
from jax.sharding import PartitionSpec as P

HID = 256
BLK = 128
HALF = 128
NR = 16
NC = 8
SPAN = 256
K = 32
MESH = pl.DeviceIdType.MESH
F32 = jnp.float32
BF16 = jnp.bfloat16


def kernel(
    owner_hbm, slot_hbm, target_hbm, nodes_hbm, w_hbm, adj_hbm, hist_hbm, tiles_hbm, cot_hbm,
    act_hbm, gn_hbm, gw_hbm,
    owner_ref, slot_ref, target_ref, act_ref, gn_ref,
    nodes_all, hist0, hist1, adj, w, cot, tiles, mix, mix_rcv, mix_snd, mix_far, mix_own, sums,
    rs_snd, rs_rcv, gt, sib_snd, sib_rcv, d_snd, d_rcv,
    gwt, gwt_snd, gw_rcv1, gw_rcv2, gw_all, chain_v, chain_ref,
    loc_sem, snd_sem, ag_sem, rs_sem, g_sem, sib_sem, d_sem, one_sem, near_sem, far_sem,
):
    r = lax.axis_index("row")
    c = lax.axis_index("col")
    core = r % 2
    chip = r // 2
    x = chip // 4
    y = chip % 4
    other = 1 - x
    up = (y + 1) % 4
    down = (y + 3) % 4
    far = (y + 2) % 4
    sib = r + 1 - 2 * core
    z = c % 4
    z_up = c - z + (z + 1) % 4
    z_down = c - z + (z + 3) % 4
    c_across = (c + 4) % NC

    def row_of(xx, yy, kk):
        return (xx * 4 + yy) * 2 + kk

    hist = (hist0, hist1)
    groups = dict(mixz=3, mixx=15, rs0=4, rs1=5, g0=6, g1=7, sib0=8, sib1=9, d0=10, d1=11, w1=12, w2=13, w3=14)
    col_order = [
        ((c // 4 + dx) % 2) * 4 + (z + dz) % 4
        for dx, dz in ((1, 2), (0, 2), (1, 1), (0, 1), (1, 3), (0, 3), (1, 0))
    ]

    def copy_of(src, dst, group, rsem, row, col):
        return pltpu.make_async_remote_copy(
            src_ref=src, dst_ref=dst, send_sem=snd_sem.at[groups.get(group, group)], recv_sem=rsem,
            device_id=(row, col), device_id_type=MESH,
        )

    def send(src, dst, group, rsem, row, col):
        copy_of(src, dst, group, rsem, row, col).start()

    def arrive(dst, rsem):
        copy_of(dst, dst, 0, rsem, sib, c).wait_recv()

    def all_sent(src, group):
        copy_of(src, src, group, one_sem.at[0], sib, c).wait_send()

    def local(src, dst, i):
        copy = pltpu.make_async_copy(src, dst, loc_sem.at[i])
        copy.start()
        return copy

    def span(i):
        return pl.ds(pl.multiple_of(i * SPAN, SPAN), SPAN)

    own_nodes = local(nodes_hbm, nodes_all.at[span(r)], 0)
    own_hist = [
        local(hist_hbm.at[:, :, pl.ds(h * HALF, HALF)], hist[h].at[pl.ds(r * 8, 8)], 1 + h)
        for h in range(2)
    ]
    w_copy = local(w_hbm, w, 3)
    adj_copy = local(adj_hbm, adj, 4)
    tiles_copy = local(tiles_hbm, tiles, 5)
    cot_copy = local(cot_hbm, cot, 6)
    pull_copies = [
        local(src, dst, 8 + i)
        for i, (src, dst) in enumerate(
            ((target_hbm, target_ref), (owner_hbm, owner_ref), (slot_hbm, slot_ref))
        )
    ]

    barrier = pltpu.get_barrier_semaphore()
    for rr, cc in (
        (row_of(other, y, core), c), (row_of(x, up, core), c), (row_of(x, down, core), c), (sib, c),
        (r, z_up), (r, z_down), (r, c_across),
    ):
        pl.semaphore_signal(barrier, inc=1, device_id=(rr, cc), device_id_type=MESH)
    pl.semaphore_wait(barrier, 7)

    def piece(chunk, owner, part):
        if chunk == 0:
            if part is None:
                return nodes_all.at[span(owner)]
            return nodes_all.at[pl.ds(pl.multiple_of(owner * SPAN + part * 128, 128), 128)]
        if part is None:
            return hist[chunk - 1].at[pl.ds(owner * 8, 8)]
        return hist[chunk - 1].at[pl.ds(owner * 8 + part * 4, 4)]

    def push(chunk, owner, part, dest):
        ref = piece(chunk, owner, part)
        send(ref, ref, chunk, ag_sem.at[chunk, owner, part or 0], dest, c)

    def got(chunk, owner, part=None):
        arrive(piece(chunk, owner, part), ag_sem.at[chunk, owner, part or 0])

    def own_y(chunk):
        push(chunk, r, None, row_of(x, up, core))
        push(chunk, r, None, row_of(x, down, core))

    def own_x(chunk):
        push(chunk, r, None, row_of(other, y, core))
        push(chunk, r, None, sib)

    def step_a(chunk):
        o = row_of(other, y, core)
        got(chunk, o)
        push(chunk, o, None, row_of(x, up, core))
        push(chunk, o, None, row_of(x, down, core))
        push(chunk, o, None, sib)

    def step_b(chunk):
        o = row_of(x, down, core)
        got(chunk, o)
        push(chunk, o, 0, row_of(x, up, core))
        push(chunk, o, None, sib)
        o = row_of(x, up, core)
        got(chunk, o)
        push(chunk, o, 1, row_of(x, down, core))
        push(chunk, o, None, sib)

    def step_c(chunk):
        for yy in (down, up):
            o = row_of(other, yy, core)
            got(chunk, o)
            push(chunk, o, None, sib)

    def step_d(chunk):
        o = row_of(x, far, core)
        for part in range(2):
            got(chunk, o, part)
            push(chunk, o, part, row_of(other, y, core))
            push(chunk, o, part, sib)

    def step_e(chunk):
        o = row_of(other, far, core)
        for part in range(2):
            got(chunk, o, part)
            push(chunk, o, part, sib)

    def step_f(chunk):
        k = 1 - core
        for xx, yy in ((x, y), (other, y), (x, down), (x, up), (other, down), (other, up)):
            got(chunk, row_of(xx, yy, k))
        for xx in (x, other):
            for part in range(2):
                got(chunk, row_of(xx, far, k), part)

    def make_chain():
        lane = lax.broadcasted_iota(jnp.int32, (K, 128), 1)
        sub = lax.broadcasted_iota(jnp.int32, (K, 128), 0)
        ask, mine = lane - K, sub
        for k in range(K):
            t = target_ref[k]
            ask = jnp.where(lane == k, t, ask)
            mine = jnp.where(sub == k, t, mine)
        match = (mine == ask) & (sub < jnp.minimum(lane, K))
        chain_v[...] = jnp.max(jnp.where(match, sub + 1, 0), axis=0, keepdims=True)
        return local(chain_v, chain_ref, 7)

    def forward_piece(i):
        rows = pl.ds(i * 512, 512)
        mix[rows, :] = jnp.dot(
            adj[rows, :], nodes_all[...], preferred_element_type=F32
        ).astype(BF16)

    def scatter_mix():
        for dz in (2, 1, 3):
            zz = (z + dz) % 4
            for xx in range(2):
                send(
                    mix.at[span(xx * 4 + zz)], mix_rcv.at[z, xx], "mixz", one_sem.at[0],
                    r, c - z + zz,
                )

    def cross_mix():
        arrive(mix_rcv.at[pl.ds(0, 3)], one_sem.at[0])
        xx = c // 4
        theirs = mix[span((1 - xx) * 4 + z), :].astype(F32)
        for dz in range(1, 4):
            theirs = theirs + mix_rcv[(z + dz) % 4, 1 - xx].astype(F32)
        mix_snd[...] = theirs.astype(BF16)
        send(mix_snd, mix_far, "mixx", one_sem.at[4], r, c_across)

    def collect_mix():
        xx = c // 4
        total = mix[span(c), :].astype(F32)
        for dz in range(1, 4):
            total = total + mix_rcv[(z + dz) % 4, xx].astype(F32)
        arrive(mix_far, one_sem.at[4])
        mix_own[...] = (total + mix_far[...].astype(F32)).astype(BF16)

    def history_and_scatter(h):
        sums[0] = jnp.zeros((BLK, HALF), F32)

        def product(k, carry):
            block = hist[h][owner_ref[k] * 8 + slot_ref[k]]
            sums[k + 1] = jnp.dot(tiles[k], block, preferred_element_type=F32)
            return carry

        lax.fori_loop(0, K, product, 0, unroll=8)

        def link(k, carry):
            sums[k + 1] = sums[k + 1] + sums[chain_ref[0, k]]
            return carry

        lax.fori_loop(0, K, link, 0, unroll=4)
        for cc in col_order + [c]:
            for i in range(2):
                v = sums[chain_ref[0, K + cc * 2 + i]]
                rs_snd[h, cc, pl.ds(i * BLK, BLK), :] = v.astype(BF16)
            if cc is not c:
                send(rs_snd.at[h, cc], rs_rcv.at[h, c], f"rs{h}", rs_sem.at[h], r, cc)

    def activate(h):
        cols = pl.ds(h * HALF, HALF)
        mixed = jnp.dot(mix_own[...], w[:, cols], preferred_element_type=F32)
        mixed = mixed + rs_snd[h, c].astype(F32)
        arrive(rs_rcv.at[h, pl.ds(0, NC - 1)], rs_sem.at[h])
        for cc in col_order:
            mixed = mixed + rs_rcv[h, cc].astype(F32)
        s = 1.0 / (1.0 + jnp.exp(-mixed))
        g = cot[:, cols].astype(F32) * s * (1.0 + mixed * (1.0 - s))
        g = g.T.astype(BF16)
        own = gt.at[h, :, span(c)]
        own[...] = g
        for cc in col_order:
            send(own, own, f"g{h}", g_sem.at[h], r, cc)
        term = jnp.dot(g, mix_own[...], preferred_element_type=F32)
        gwt[pl.ds(h * HALF, HALF), :] = term
        gwt_snd[pl.ds(h * HALF, HALF), :] = term.astype(BF16)
        act_ref[:, cols] = (mixed * s).astype(BF16)

    def near(i):
        return ((x + 1 - i % 2) % 2) * 4 + (y + 3 - i // 2) % 4

    def sib_copy(h, q):
        return copy_of(sib_snd.at[h, q], sib_rcv.at[h, q], f"sib{h}", sib_sem.at[h, q], sib, c)

    def row_copy(h, q):
        return copy_of(
            d_snd.at[h, q], d_rcv.at[h, chip], f"d{h}", d_sem.at[h], q * 2 + core, c
        )

    def backward(h):
        arrive(gt.at[h, :, pl.ds(0, (NC - 1) * SPAN)], g_sem.at[h])

        def for_sib(i, carry):
            q = near(i)
            v = jnp.dot(gt[h], adj[:, span(2 * q + 1 - core)], preferred_element_type=F32)
            sib_snd[h, q] = v.astype(BF16)
            sib_copy(h, q).start()
            return carry

        lax.fori_loop(0, 8, for_sib, 0)

        def summed(q):
            v = jnp.dot(gt[h], adj[:, span(2 * q + core)], preferred_element_type=F32)
            arrive(sib_rcv.at[h, q], sib_sem.at[h, q])
            d_snd[h, q] = (v + sib_rcv[h, q].astype(F32)).astype(BF16)

        def for_chip(i, carry):
            q = near(i)
            summed(q)
            row_copy(h, q).start()
            return carry

        lax.fori_loop(0, 7, for_chip, 0)
        summed(chip)

    def collect_rows(h):
        arrive(d_rcv.at[h, pl.ds(0, 7)], d_sem.at[h])
        total = d_snd[h, chip].astype(F32)
        for d in range(1, 8):
            total = total + d_rcv[h, (chip + d) % 8].astype(F32)
        return lax.dot_general(
            total.T.astype(BF16), w[:, pl.ds(h * HALF, HALF)], (((1,), (1,)), ((), ())),
            preferred_element_type=F32,
        )

    def weight_rows(i):
        return pl.ds(pl.multiple_of(i * 16, 16), 16)

    own_nodes.wait()
    own_y(0)
    own_x(0)
    own_hist[0].wait()
    own_y(1)
    own_x(1)
    for cc in (z_up, z_down):
        pl.semaphore_signal(near_sem, inc=1, device_id=(r, cc), device_id_type=MESH)
    own_hist[1].wait()
    for copy in pull_copies:
        copy.wait()
    chain_copy = make_chain()
    step_b(0)
    step_a(0)
    own_x(2)
    pl.semaphore_wait(near_sem, 2)
    pl.semaphore_signal(far_sem, inc=1, device_id=(r, c_across), device_id_type=MESH)
    step_c(0)
    step_d(0)
    step_b(1)
    own_y(2)
    step_a(1)
    step_e(0)
    step_f(0)
    w_copy.wait()
    adj_copy.wait()
    forward_piece(0)
    forward_piece(1)
    step_d(1)
    forward_piece(2)
    forward_piece(3)
    pl.semaphore_wait(far_sem, 1)
    scatter_mix()
    step_b(2)
    step_a(2)
    step_e(1)
    step_c(1)
    tiles_copy.wait()
    cot_copy.wait()
    chain_copy.wait()
    step_f(1)
    history_and_scatter(0)
    step_d(2)
    step_c(2)
    cross_mix()
    step_e(2)
    step_f(2)
    history_and_scatter(1)
    collect_mix()
    activate(0)
    activate(1)
    act_copy = local(act_ref, act_hbm, 11)
    for d in range(1, NR):
        rr = (r + d) % NR
        send(gwt_snd.at[weight_rows(rr)], gw_rcv1.at[r], "w1", one_sem.at[1], rr, c)
    backward(0)
    arrive(gw_rcv1.at[pl.ds(0, NR - 1)], one_sem.at[1])
    total = gwt[weight_rows(r), :]
    for d in range(1, NR):
        total = total + gw_rcv1[(r + d) % NR].astype(F32)
    gw_rcv2[c] = total.astype(BF16)
    for cc in col_order:
        send(gw_rcv2.at[c], gw_rcv2.at[c], "w2", one_sem.at[2], r, cc)
    backward(1)
    arrive(gw_rcv2.at[pl.ds(0, NC - 1)], one_sem.at[2])
    total = gw_rcv2[0].astype(F32)
    for i in range(1, NC):
        total = total + gw_rcv2[i].astype(F32)
    gw_all[r] = total.astype(BF16)
    for d in range(1, NR):
        send(gw_all.at[r], gw_all.at[r], "w3", one_sem.at[3], (r + d) % NR, c)
    part = collect_rows(0)
    gn_ref[...] = (part + collect_rows(1)).astype(BF16)
    gn_copy = local(gn_ref, gn_hbm, 12)
    arrive(gw_all.at[pl.ds(0, NR - 1)], one_sem.at[3])
    gw_copy = local(gw_all, gw_hbm, 13)
    all_sent(nodes_all.at[pl.ds(0, 15 * SPAN)], 0)
    for h in range(2):
        all_sent(hist[h].at[pl.ds(0, 120)], 1 + h)
        all_sent(rs_snd.at[h, pl.ds(0, NC - 1)], f"rs{h}")
        all_sent(gt.at[h, :, pl.ds(0, (NC - 1) * SPAN)], f"g{h}")
        all_sent(sib_snd.at[h], f"sib{h}")
        all_sent(d_snd.at[h, pl.ds(0, 7)], f"d{h}")
    all_sent(mix.at[pl.ds(0, 6 * SPAN)], "mixz")
    all_sent(mix_snd, "mixx")
    all_sent(gwt_snd.at[pl.ds(0, (NR - 1) * 16)], "w1")
    all_sent(gw_rcv2.at[pl.ds(0, NC - 1)], "w2")
    all_sent(gw_all.at[pl.ds(0, NR - 1)], "w3")
    for copy in (act_copy, gn_copy, gw_copy):
        copy.wait()


def finish(scale, act_ref, gn_ref, gw_ref, act_out, gn_out, gw_out):
    act_out[...] = act_ref[...]
    gn_out[...] = gn_ref[...]
    gw_out[...] = gw_ref[...].astype(F32).T * scale


def local(
    nodes, weight, adjacency, history, pull_owner, pull_slot, pull_target, hist_tiles, cotangent
):
    any_ = pl.BlockSpec(memory_space=pl.ANY)
    vmem = pl.BlockSpec(memory_space=pltpu.VMEM)
    dma = pltpu.SemaphoreType.DMA
    act, grad_nodes, gw = pl.pallas_call(
        kernel,
        out_shape=(
            jax.ShapeDtypeStruct((SPAN, HID), BF16),
            jax.ShapeDtypeStruct((SPAN, HID), BF16),
            jax.ShapeDtypeStruct((NR, 16, HID), BF16),
        ),
        in_specs=[any_] * 9,
        out_specs=(any_,) * 3,
        scratch_shapes=[
            pltpu.SMEM((K,), jnp.int32),
            pltpu.SMEM((K,), jnp.int32),
            pltpu.SMEM((K,), jnp.int32),
            pltpu.VMEM((SPAN, HID), BF16),
            pltpu.VMEM((SPAN, HID), BF16),
            pltpu.VMEM((4096, HID), BF16),
            pltpu.VMEM((128, BLK, HALF), BF16),
            pltpu.VMEM((128, BLK, HALF), BF16),
            pltpu.VMEM((2048, 4096), BF16),
            pltpu.VMEM((HID, HID), BF16),
            pltpu.VMEM((SPAN, HID), BF16),
            pltpu.VMEM((K, BLK, BLK), BF16),
            pltpu.VMEM((2048, HID), BF16),
            pltpu.VMEM((4, 2, SPAN, HID), BF16),
            pltpu.VMEM((SPAN, HID), BF16),
            pltpu.VMEM((SPAN, HID), BF16),
            pltpu.VMEM((SPAN, HID), BF16),
            pltpu.VMEM((K + 1, BLK, HALF), F32),
            pltpu.VMEM((2, NC, SPAN, HALF), BF16),
            pltpu.VMEM((2, NC, SPAN, HALF), BF16),
            pltpu.VMEM((2, HALF, 2048), BF16),
            pltpu.VMEM((2, 8, HALF, SPAN), BF16),
            pltpu.VMEM((2, 8, HALF, SPAN), BF16),
            pltpu.VMEM((2, 8, HALF, SPAN), BF16),
            pltpu.VMEM((2, 8, HALF, SPAN), BF16),
            pltpu.VMEM((HID, HID), F32),
            pltpu.VMEM((HID, HID), BF16),
            pltpu.VMEM((NR, 16, HID), BF16),
            pltpu.VMEM((NC, 16, HID), BF16),
            pltpu.VMEM((NR, 16, HID), BF16),
            pltpu.VMEM((1, 128), jnp.int32),
            pltpu.SMEM((1, 128), jnp.int32),
            dma((14,)),
            dma((16,)),
            dma((3, NR, 2)),
            dma((2,)),
            dma((2,)),
            dma((2, 8)),
            dma((2,)),
            dma((5,)),
            pltpu.SemaphoreType.REGULAR,
            pltpu.SemaphoreType.REGULAR,
        ],
        compiler_params=pltpu.CompilerParams(
            collective_id=0, has_side_effects=True, vmem_limit_bytes=60 * 2**20
        ),
    )(
        pull_owner[:, 0], pull_slot, pull_target, nodes, weight, adjacency,
        history.reshape(8, BLK, HID), hist_tiles, cotangent,
    )
    all_nodes = nodes.shape[0] * NR * NC
    return pl.pallas_call(
        lambda *refs: finish(1.0 / math.sqrt(all_nodes), *refs),
        out_shape=(
            jax.ShapeDtypeStruct((SPAN, HID), BF16),
            jax.ShapeDtypeStruct((SPAN, HID), BF16),
            jax.ShapeDtypeStruct((HID, HID), F32),
        ),
        in_specs=[vmem] * 3,
        out_specs=(vmem,) * 3,
    )(act, grad_nodes, gw.reshape(HID, HID))


def solution(mesh):
    return jax.shard_map(
        local,
        mesh=mesh,
        in_specs=(
            P(("row", "col"), None),
            P(),
            P("row", "col"),
            P(("row", "col"), None),
            P(("row", "col"), None),
            P(("row", "col")),
            P(("row", "col")),
            P(("row", "col"), None, None),
            P(("row", "col"), None),
        ),
        out_specs=(P(("row", "col"), None), P(("row", "col"), None), P()),
        check_vma=False,
    )
```

```python
import math

import jax
import jax.numpy as jnp
from jax import lax
from jax.experimental import pallas as pl
from jax.experimental.pallas import tpu as pltpu
from jax.sharding import PartitionSpec as P

HID = 256
BLK = 128
HALF = 128
NR = 16
NC = 8
SPAN = 256
K = 32
MESH = pl.DeviceIdType.MESH
F32 = jnp.float32
BF16 = jnp.bfloat16


def kernel(
    owner_hbm, slot_hbm, target_hbm, nodes_hbm, w_hbm, adj_hbm, hist_hbm, tiles_hbm, cot_hbm,
    act_hbm, gn_hbm, gw_hbm,
    owner_ref, slot_ref, target_ref, act_ref, gn_ref,
    nodes_all, hist0, hist1, adj, w, cot, tiles, mix, mix_rcv, mix_snd, mix_far, mix_own, sums,
    rs_snd, rs_rcv, gt, sib_snd, sib_rcv, d_snd, d_rcv,
    gwt, gwt_snd, gw_rcv1, gw_rcv2, gw_all, chain_v, chain_ref,
    loc_sem, snd_sem, ag_sem, rs_sem, g_sem, sib_sem, d_sem, one_sem, near_sem, far_sem,
):
    r = lax.axis_index("row")
    c = lax.axis_index("col")
    core = r % 2
    chip = r // 2
    x = chip // 4
    y = chip % 4
    other = 1 - x
    up = (y + 1) % 4
    down = (y + 3) % 4
    far = (y + 2) % 4
    sib = r + 1 - 2 * core
    z = c % 4
    z_up = c - z + (z + 1) % 4
    z_down = c - z + (z + 3) % 4
    c_across = (c + 4) % NC

    def row_of(xx, yy, kk):
        return (xx * 4 + yy) * 2 + kk

    hist = (hist0, hist1)
    groups = dict(mixz=3, mixx=15, rs0=4, rs1=5, g0=6, g1=7, sib0=8, sib1=9, d0=10, d1=11, w1=12, w2=13, w3=14)
    col_order = [
        ((c // 4 + dx) % 2) * 4 + (z + dz) % 4
        for dx, dz in ((1, 2), (0, 2), (1, 1), (0, 1), (1, 3), (0, 3), (1, 0))
    ]

    row_order = [
        row_of((x + dx) % 2, (y + dy) % 4, (core + dk) % 2)
        for dx, dy in ((1, 2), (0, 2), (1, 1), (0, 1), (1, 3), (0, 3), (1, 0), (0, 0))
        for dk in range(2)
        if dx or dy or dk
    ]

    def copy_of(src, dst, group, rsem, row, col):
        return pltpu.make_async_remote_copy(
            src_ref=src, dst_ref=dst, send_sem=snd_sem.at[groups.get(group, group)], recv_sem=rsem,
            device_id=(row, col), device_id_type=MESH,
        )

    def send(src, dst, group, rsem, row, col):
        copy_of(src, dst, group, rsem, row, col).start()

    def arrive(dst, rsem):
        copy_of(dst, dst, 0, rsem, sib, c).wait_recv()

    def all_sent(src, group):
        copy_of(src, src, group, one_sem.at[0], sib, c).wait_send()

    def local(src, dst, i):
        copy = pltpu.make_async_copy(src, dst, loc_sem.at[i])
        copy.start()
        return copy

    def span(i):
        return pl.ds(pl.multiple_of(i * SPAN, SPAN), SPAN)

    own_nodes = local(nodes_hbm, nodes_all.at[span(r)], 0)
    own_hist = [
        local(hist_hbm.at[:, :, pl.ds(h * HALF, HALF)], hist[h].at[pl.ds(r * 8, 8)], 1 + h)
        for h in range(2)
    ]
    w_copy = local(w_hbm, w, 3)
    adj_copy = local(adj_hbm, adj, 4)
    tiles_copy = local(tiles_hbm, tiles, 5)
    cot_copy = local(cot_hbm, cot, 6)
    pull_copies = [
        local(src, dst, 8 + i)
        for i, (src, dst) in enumerate(
            ((target_hbm, target_ref), (owner_hbm, owner_ref), (slot_hbm, slot_ref))
        )
    ]

    barrier = pltpu.get_barrier_semaphore()
    for rr, cc in (
        (row_of(other, y, core), c), (row_of(x, up, core), c), (row_of(x, down, core), c), (sib, c),
        (r, z_up), (r, z_down), (r, c_across),
    ):
        pl.semaphore_signal(barrier, inc=1, device_id=(rr, cc), device_id_type=MESH)
    pl.semaphore_wait(barrier, 7)

    def piece(chunk, owner, part):
        if chunk == 0:
            if part is None:
                return nodes_all.at[span(owner)]
            return nodes_all.at[pl.ds(pl.multiple_of(owner * SPAN + part * 128, 128), 128)]
        if part is None:
            return hist[chunk - 1].at[pl.ds(owner * 8, 8)]
        return hist[chunk - 1].at[pl.ds(owner * 8 + part * 4, 4)]

    def push(chunk, owner, part, dest):
        ref = piece(chunk, owner, part)
        send(ref, ref, chunk, ag_sem.at[chunk, owner, part or 0], dest, c)

    def got(chunk, owner, part=None):
        arrive(piece(chunk, owner, part), ag_sem.at[chunk, owner, part or 0])

    def own_y(chunk):
        push(chunk, r, None, row_of(x, up, core))
        push(chunk, r, None, row_of(x, down, core))

    def own_x(chunk):
        push(chunk, r, None, row_of(other, y, core))
        push(chunk, r, None, sib)

    def step_a(chunk):
        o = row_of(other, y, core)
        got(chunk, o)
        push(chunk, o, None, row_of(x, up, core))
        push(chunk, o, None, row_of(x, down, core))
        push(chunk, o, None, sib)

    def step_b(chunk):
        o = row_of(x, down, core)
        got(chunk, o)
        push(chunk, o, 0, row_of(x, up, core))
        push(chunk, o, None, sib)
        o = row_of(x, up, core)
        got(chunk, o)
        push(chunk, o, 1, row_of(x, down, core))
        push(chunk, o, None, sib)

    def step_c(chunk):
        for yy in (down, up):
            o = row_of(other, yy, core)
            got(chunk, o)
            push(chunk, o, None, sib)

    def step_d(chunk):
        o = row_of(x, far, core)
        for part in range(2):
            got(chunk, o, part)
            push(chunk, o, part, row_of(other, y, core))
            push(chunk, o, part, sib)

    def step_e(chunk):
        o = row_of(other, far, core)
        for part in range(2):
            got(chunk, o, part)
            push(chunk, o, part, sib)

    def step_f(chunk):
        k = 1 - core
        for xx, yy in ((x, y), (other, y), (x, down), (x, up), (other, down), (other, up)):
            got(chunk, row_of(xx, yy, k))
        for xx in (x, other):
            for part in range(2):
                got(chunk, row_of(xx, far, k), part)

    def make_chain():
        lane = lax.broadcasted_iota(jnp.int32, (K, 128), 1)
        sub = lax.broadcasted_iota(jnp.int32, (K, 128), 0)
        ask, mine = lane - K, sub
        for k in range(K):
            t = target_ref[k]
            ask = jnp.where(lane == k, t, ask)
            mine = jnp.where(sub == k, t, mine)
        match = (mine == ask) & (sub < jnp.minimum(lane, K))
        chain_v[...] = jnp.max(jnp.where(match, sub + 1, 0), axis=0, keepdims=True)
        return local(chain_v, chain_ref, 7)

    def forward_piece(i):
        rows = pl.ds(i * 512, 512)
        mix[rows, :] = jnp.dot(
            adj[rows, :], nodes_all[...], preferred_element_type=F32
        ).astype(BF16)

    def scatter_mix():
        for dz in (2, 1, 3):
            zz = (z + dz) % 4
            for xx in range(2):
                send(
                    mix.at[span(xx * 4 + zz)], mix_rcv.at[z, xx], "mixz", one_sem.at[0],
                    r, c - z + zz,
                )

    def cross_mix():
        arrive(mix_rcv.at[pl.ds(0, 3)], one_sem.at[0])
        xx = c // 4
        theirs = mix[span((1 - xx) * 4 + z), :].astype(F32)
        for dz in range(1, 4):
            theirs = theirs + mix_rcv[(z + dz) % 4, 1 - xx].astype(F32)
        mix_snd[...] = theirs.astype(BF16)
        send(mix_snd, mix_far, "mixx", one_sem.at[4], r, c_across)

    def collect_mix():
        xx = c // 4
        total = mix[span(c), :].astype(F32)
        for dz in range(1, 4):
            total = total + mix_rcv[(z + dz) % 4, xx].astype(F32)
        arrive(mix_far, one_sem.at[4])
        mix_own[...] = (total + mix_far[...].astype(F32)).astype(BF16)

    def history_and_scatter(h):
        sums[0] = jnp.zeros((BLK, HALF), F32)

        def product(k, carry):
            block = hist[h][owner_ref[k] * 8 + slot_ref[k]]
            sums[k + 1] = jnp.dot(tiles[k], block, preferred_element_type=F32)
            return carry

        lax.fori_loop(0, K, product, 0, unroll=16)

        def link(k, carry):
            sums[k + 1] = sums[k + 1] + sums[chain_ref[0, k]]
            return carry

        lax.fori_loop(0, K, link, 0, unroll=8)
        for cc in col_order + [c]:
            for i in range(2):
                v = sums[chain_ref[0, K + cc * 2 + i]]
                rs_snd[h, cc, pl.ds(i * BLK, BLK), :] = v.astype(BF16)
            if cc is not c:
                send(rs_snd.at[h, cc], rs_rcv.at[h, c], f"rs{h}", rs_sem.at[h], r, cc)

    def activate(h):
        cols = pl.ds(h * HALF, HALF)
        mixed = jnp.dot(mix_own[...], w[:, cols], preferred_element_type=F32)
        mixed = mixed + rs_snd[h, c].astype(F32)
        arrive(rs_rcv.at[h, pl.ds(0, NC - 1)], rs_sem.at[h])
        for cc in col_order:
            mixed = mixed + rs_rcv[h, cc].astype(F32)
        s = 1.0 / (1.0 + jnp.exp(-mixed))
        g = cot[:, cols].astype(F32) * s * (1.0 + mixed * (1.0 - s))
        g = g.T.astype(BF16)
        own = gt.at[h, :, span(c)]
        own[...] = g
        for cc in col_order:
            send(own, own, f"g{h}", g_sem.at[h], r, cc)
        term = jnp.dot(g, mix_own[...], preferred_element_type=F32)
        gwt[pl.ds(h * HALF, HALF), :] = term
        gwt_snd[pl.ds(h * HALF, HALF), :] = term.astype(BF16)
        act_ref[:, cols] = (mixed * s).astype(BF16)

    def near(i):
        return ((x + 1 - i % 2) % 2) * 4 + (y + 3 - i // 2) % 4

    def sib_copy(h, q):
        return copy_of(sib_snd.at[h, q], sib_rcv.at[h, q], f"sib{h}", sib_sem.at[h, q], sib, c)

    def row_copy(h, q):
        return copy_of(
            d_snd.at[h, q], d_rcv.at[h, chip], f"d{h}", d_sem.at[h], q * 2 + core, c
        )

    def backward(h):
        arrive(gt.at[h, :, pl.ds(0, (NC - 1) * SPAN)], g_sem.at[h])

        def for_sib(i, carry):
            q = near(i)
            v = jnp.dot(gt[h], adj[:, span(2 * q + 1 - core)], preferred_element_type=F32)
            sib_snd[h, q] = v.astype(BF16)
            sib_copy(h, q).start()
            return carry

        lax.fori_loop(0, 8, for_sib, 0)

        def summed(q):
            v = jnp.dot(gt[h], adj[:, span(2 * q + core)], preferred_element_type=F32)
            arrive(sib_rcv.at[h, q], sib_sem.at[h, q])
            d_snd[h, q] = (v + sib_rcv[h, q].astype(F32)).astype(BF16)

        def for_chip(i, carry):
            q = near(i)
            summed(q)
            row_copy(h, q).start()
            return carry

        lax.fori_loop(0, 7, for_chip, 0)
        summed(chip)

    def collect_rows(h):
        arrive(d_rcv.at[h, pl.ds(0, 7)], d_sem.at[h])
        total = d_snd[h, chip].astype(F32)
        for d in range(1, 8):
            total = total + d_rcv[h, (chip + d) % 8].astype(F32)
        return lax.dot_general(
            total.T.astype(BF16), w[:, pl.ds(h * HALF, HALF)], (((1,), (1,)), ((), ())),
            preferred_element_type=F32,
        )

    def weight_rows(i):
        return pl.ds(pl.multiple_of(i * 16, 16), 16)

    own_nodes.wait()
    own_y(0)
    own_x(0)
    own_hist[0].wait()
    own_y(1)
    own_x(1)
    for cc in (z_up, z_down):
        pl.semaphore_signal(near_sem, inc=1, device_id=(r, cc), device_id_type=MESH)
    own_hist[1].wait()
    for copy in pull_copies:
        copy.wait()
    chain_copy = make_chain()
    step_b(0)
    step_a(0)
    own_x(2)
    pl.semaphore_wait(near_sem, 2)
    pl.semaphore_signal(far_sem, inc=1, device_id=(r, c_across), device_id_type=MESH)
    step_c(0)
    step_d(0)
    step_b(1)
    own_y(2)
    step_a(1)
    step_e(0)
    step_f(0)
    w_copy.wait()
    adj_copy.wait()
    forward_piece(0)
    forward_piece(1)
    step_d(1)
    forward_piece(2)
    forward_piece(3)
    pl.semaphore_wait(far_sem, 1)
    scatter_mix()
    step_b(2)
    step_a(2)
    step_e(1)
    step_c(1)
    tiles_copy.wait()
    cot_copy.wait()
    chain_copy.wait()
    step_f(1)
    history_and_scatter(0)
    step_d(2)
    step_c(2)
    cross_mix()
    step_e(2)
    step_f(2)
    history_and_scatter(1)
    collect_mix()
    activate(0)
    activate(1)
    act_copy = local(act_ref, act_hbm, 11)
    for rr in row_order:
        send(gwt_snd.at[weight_rows(rr)], gw_rcv1.at[r], "w1", one_sem.at[1], rr, c)
    backward(0)
    arrive(gw_rcv1.at[pl.ds(0, NR - 1)], one_sem.at[1])
    total = gwt[weight_rows(r), :]
    for d in range(1, NR):
        total = total + gw_rcv1[(r + d) % NR].astype(F32)
    gw_rcv2[c] = total.astype(BF16)
    for cc in col_order:
        send(gw_rcv2.at[c], gw_rcv2.at[c], "w2", one_sem.at[2], r, cc)
    backward(1)
    arrive(gw_rcv2.at[pl.ds(0, NC - 1)], one_sem.at[2])
    total = gw_rcv2[0].astype(F32)
    for i in range(1, NC):
        total = total + gw_rcv2[i].astype(F32)
    gw_all[r] = total.astype(BF16)
    for rr in row_order:
        send(gw_all.at[r], gw_all.at[r], "w3", one_sem.at[3], rr, c)
    part = collect_rows(0)
    gn_ref[...] = (part + collect_rows(1)).astype(BF16)
    gn_copy = local(gn_ref, gn_hbm, 12)
    arrive(gw_all.at[pl.ds(0, NR - 1)], one_sem.at[3])
    gw_copy = local(gw_all, gw_hbm, 13)
    all_sent(nodes_all.at[pl.ds(0, 15 * SPAN)], 0)
    for h in range(2):
        all_sent(hist[h].at[pl.ds(0, 120)], 1 + h)
        all_sent(rs_snd.at[h, pl.ds(0, NC - 1)], f"rs{h}")
        all_sent(gt.at[h, :, pl.ds(0, (NC - 1) * SPAN)], f"g{h}")
        all_sent(sib_snd.at[h], f"sib{h}")
        all_sent(d_snd.at[h, pl.ds(0, 7)], f"d{h}")
    all_sent(mix.at[pl.ds(0, 6 * SPAN)], "mixz")
    all_sent(mix_snd, "mixx")
    all_sent(gwt_snd.at[pl.ds(0, (NR - 1) * 16)], "w1")
    all_sent(gw_rcv2.at[pl.ds(0, NC - 1)], "w2")
    all_sent(gw_all.at[pl.ds(0, NR - 1)], "w3")
    for copy in (act_copy, gn_copy, gw_copy):
        copy.wait()


def finish(scale, act_ref, gn_ref, gw_ref, act_out, gn_out, gw_out):
    act_out[...] = act_ref[...]
    gn_out[...] = gn_ref[...]
    gw_out[...] = gw_ref[...].astype(F32).T * scale


def local(
    nodes, weight, adjacency, history, pull_owner, pull_slot, pull_target, hist_tiles, cotangent
):
    any_ = pl.BlockSpec(memory_space=pl.ANY)
    vmem = pl.BlockSpec(memory_space=pltpu.VMEM)
    dma = pltpu.SemaphoreType.DMA
    act, grad_nodes, gw = pl.pallas_call(
        kernel,
        out_shape=(
            jax.ShapeDtypeStruct((SPAN, HID), BF16),
            jax.ShapeDtypeStruct((SPAN, HID), BF16),
            jax.ShapeDtypeStruct((NR, 16, HID), BF16),
        ),
        in_specs=[any_] * 9,
        out_specs=(any_,) * 3,
        scratch_shapes=[
            pltpu.SMEM((K,), jnp.int32),
            pltpu.SMEM((K,), jnp.int32),
            pltpu.SMEM((K,), jnp.int32),
            pltpu.VMEM((SPAN, HID), BF16),
            pltpu.VMEM((SPAN, HID), BF16),
            pltpu.VMEM((4096, HID), BF16),
            pltpu.VMEM((128, BLK, HALF), BF16),
            pltpu.VMEM((128, BLK, HALF), BF16),
            pltpu.VMEM((2048, 4096), BF16),
            pltpu.VMEM((HID, HID), BF16),
            pltpu.VMEM((SPAN, HID), BF16),
            pltpu.VMEM((K, BLK, BLK), BF16),
            pltpu.VMEM((2048, HID), BF16),
            pltpu.VMEM((4, 2, SPAN, HID), BF16),
            pltpu.VMEM((SPAN, HID), BF16),
            pltpu.VMEM((SPAN, HID), BF16),
            pltpu.VMEM((SPAN, HID), BF16),
            pltpu.VMEM((K + 1, BLK, HALF), F32),
            pltpu.VMEM((2, NC, SPAN, HALF), BF16),
            pltpu.VMEM((2, NC, SPAN, HALF), BF16),
            pltpu.VMEM((2, HALF, 2048), BF16),
            pltpu.VMEM((2, 8, HALF, SPAN), BF16),
            pltpu.VMEM((2, 8, HALF, SPAN), BF16),
            pltpu.VMEM((2, 8, HALF, SPAN), BF16),
            pltpu.VMEM((2, 8, HALF, SPAN), BF16),
            pltpu.VMEM((HID, HID), F32),
            pltpu.VMEM((HID, HID), BF16),
            pltpu.VMEM((NR, 16, HID), BF16),
            pltpu.VMEM((NC, 16, HID), BF16),
            pltpu.VMEM((NR, 16, HID), BF16),
            pltpu.VMEM((1, 128), jnp.int32),
            pltpu.SMEM((1, 128), jnp.int32),
            dma((14,)),
            dma((16,)),
            dma((3, NR, 2)),
            dma((2,)),
            dma((2,)),
            dma((2, 8)),
            dma((2,)),
            dma((5,)),
            pltpu.SemaphoreType.REGULAR,
            pltpu.SemaphoreType.REGULAR,
        ],
        compiler_params=pltpu.CompilerParams(
            collective_id=0, has_side_effects=True, vmem_limit_bytes=60 * 2**20
        ),
    )(
        pull_owner[:, 0], pull_slot, pull_target, nodes, weight, adjacency,
        history.reshape(8, BLK, HID), hist_tiles, cotangent,
    )
    all_nodes = nodes.shape[0] * NR * NC
    return pl.pallas_call(
        lambda *refs: finish(1.0 / math.sqrt(all_nodes), *refs),
        out_shape=(
            jax.ShapeDtypeStruct((SPAN, HID), BF16),
            jax.ShapeDtypeStruct((SPAN, HID), BF16),
            jax.ShapeDtypeStruct((HID, HID), F32),
        ),
        in_specs=[vmem] * 3,
        out_specs=(vmem,) * 3,
    )(act, grad_nodes, gw.reshape(HID, HID))


def solution(mesh):
    return jax.shard_map(
        local,
        mesh=mesh,
        in_specs=(
            P(("row", "col"), None),
            P(),
            P("row", "col"),
            P(("row", "col"), None),
            P(("row", "col"), None),
            P(("row", "col")),
            P(("row", "col")),
            P(("row", "col"), None, None),
            P(("row", "col"), None),
        ),
        out_specs=(P(("row", "col"), None), P(("row", "col"), None), P()),
        check_vma=False,
    )
```
